32 devices in a mesh: dp: 16 (over z, y, core), vocab: 2 (over x).
Axes of the slice: x: 2, y: 2, z: 4, core: 2. Of those that a mesh axis runs over, the one named last changes fastest.
Arguments:
- hidden: bfloat16 [80, 512, 4096], P('dp', None, 'vocab'), may hold values from -256 to 256
- positions: int32 [80, 80], P('dp'), may hold values from 0 to 511, as said below
- labels: int32 [80, 80], P('dp'), may hold values from 0 to 127
- lse_rest: float32 [80, 80], P('dp'), may hold values from 2 to 10
- head: float32 [2, 64, 4096], P('vocab', 'dp'), may hold values from -1.5 to 1.5
- m_state: float32 [2, 64, 4096], P('vocab', 'dp'), may hold values from -80 to 80
- v_state: float32 [2, 64, 4096], P('vocab', 'dp'), may hold values from 0.5 to 20
Outputs:
- losses: float32 [80, 80], P('dp')
- new_head: float32 [2, 64, 4096], P('vocab', 'dp')
- new_m: float32 [2, 64, 4096], P('vocab', 'dp')
- new_v: float32 [2, 64, 4096], P('vocab', 'dp')
The draws below stay inside these ranges and needn't reach their ends.
Inputs may be any that keep to these rules, and one draw needn't show every extreme that they name: The 80 positions of a sequence are distinct and ascending.
All inputs are finite; a program needn't handle non-finite values.
Results may differ from the reference program's by a relative error of at most 0.00066.
Values may be sent and summed in bfloat16 or wider, within the bound.
A program may use at most 64 MiB of HBM per device.

```python
import math
import jax
import jax.numpy as jnp
import numpy as np
from jax import lax

D = 4096
LEN = 512
MASK = 80
STEP = 100
SLAB = 64
SLABS = 2
BLOCK = 128
SEQS = 80
ROWS = 6400


def mask_positions(key):
    seq_keys = jax.random.split(jax.random.fold_in(key, 3), SEQS)
    shuffled = jax.vmap(lambda single: jax.random.permutation(single, LEN))(seq_keys)
    return jnp.sort(shuffled[:, :MASK], axis=1).astype(jnp.int32)


def head_values(key):
    key_rows, key_cols, key_base = jax.random.split(jax.random.fold_in(key, 7), 3)
    slab_index = jnp.arange(SLABS, dtype=jnp.float32)[:, None, None]
    row_index = jnp.arange(SLAB, dtype=jnp.float32)[None, :, None]
    row_trend = 0.4 * jnp.power(2.0, slab_index / SLABS) * jnp.power(3.0, row_index / SLAB)
    row_random = jnp.exp(jax.random.uniform(key_rows, (SLABS, SLAB, 1), jnp.float32, math.log(0.6), math.log(1.6)))
    col_scale = jnp.exp(jax.random.uniform(key_cols, (1, 1, D), jnp.float32, math.log(0.3), math.log(3.0)))
    base_values = jnp.clip(jax.random.normal(key_base, (SLABS, SLAB, D), jnp.float32), -5.0, 5.0)
    return jnp.clip(base_values * row_trend * row_random * col_scale / math.sqrt(D), -1.5, 1.5)


def draw_positions(key, part):
    return mask_positions(key)


def draw_head(key, part):
    return head_values(key)


def draw_hidden(key, part):
    spots = mask_positions(key)
    key_vals = jax.random.fold_in(jax.random.fold_in(key, 5), 0)
    key_target = jax.random.fold_in(jax.random.fold_in(key, 5), 3)
    key_strength = jax.random.fold_in(jax.random.fold_in(key, 5), 4)
    weights = head_values(key).reshape(BLOCK, D).astype(jnp.bfloat16).astype(jnp.float32)
    values = jnp.clip(jax.random.normal(key_vals, (SEQS, LEN, D), jnp.float32), -6.0, 6.0)
    targets = jax.random.randint(key_target, (SEQS,), 0, BLOCK)
    target_strength = jax.random.uniform(key_strength, (SEQS, 1), jnp.float32, 20.0, 30.0)
    chosen = weights[targets]
    chosen_sq = jnp.sum(chosen * chosen, axis=1, keepdims=True)
    planted = target_strength * chosen / chosen_sq
    values = values.at[jnp.arange(SEQS), spots[:, 1]].set(planted)
    return jnp.clip(values, -256.0, 256.0).astype(jnp.bfloat16)


def draw_m_state(key, part):
    key_base = jax.random.fold_in(jax.random.fold_in(key, 9), 0)
    row_index = jnp.arange(SLAB, dtype=jnp.float32)[None, :, None]
    row_trend = jnp.power(3.0, row_index / SLAB)
    values = jnp.clip(jax.random.normal(key_base, (SLABS, SLAB, D), jnp.float32), -5.0, 5.0) * 1.5 * row_trend
    return values


def touch_ends(entries, own_key, low, largest):
    shape = entries.shape
    place = [jax.random.randint(jax.random.fold_in(own_key, axis), (), 0, shape[axis]) for axis in range(len(shape))]
    entries = entries.at[tuple(place)].set(low)
    longest = shape.index(max(shape))
    place[longest] = (place[longest] + 1) % shape[longest]
    return entries.at[tuple(place)].set(largest)


def block_scale(own_key, dims, cuts, low, high):
    gain, own = 1.0, jax.random.fold_in(own_key, 6)
    for dim, shards_of in cuts:
        heights = jnp.exp(jax.random.uniform(jax.random.fold_in(own, dim), (shards_of,), jnp.float32, low / len(cuts), high / len(cuts)))
        gain = gain * jnp.repeat(heights, dims[dim] // shards_of).reshape([-1 if axis == dim else 1 for axis in range(len(dims))])
    return gain


def rank_bounds(number_of, lean):
    loads = [(1 << 20) // math.isqrt(rank ** lean) + 1 for rank in range(1, number_of + 1)]
    deviation = 1 + sum(loads) // (1 << 30)
    return np.cumsum(np.array([max(1, weight // deviation) for weight in loads]))


def ranked_ids(stream_key, extent, count, slope):
    grid = rank_bounds(count, slope)
    pick = jax.random.randint(jax.random.fold_in(stream_key, 1), extent, 0, int(grid[count - 1]))
    grade = jnp.searchsorted(jnp.asarray(grid, jnp.int32), pick, side="right")
    return jax.random.permutation(jax.random.fold_in(stream_key, 2), count)[grade].astype(jnp.int32)


def setup_inputs(seed: int = 0) -> dict:
    key_list = jax.random.split(jax.random.key(seed), 8)
    return {
        "hidden": draw_hidden(jax.random.fold_in(key_list[7], 71), 0),
        "positions": draw_positions(jax.random.fold_in(key_list[7], 71), 0),
        "labels": touch_ends(ranked_ids(key_list[2], (SEQS, MASK), BLOCK, 2), jax.random.fold_in(key_list[2], 3), 0, BLOCK - 1).astype(jnp.int32),
        "lse_rest": jnp.clip(2.0 + 8.0 * jax.random.uniform(key_list[3], (SEQS, MASK), jnp.float32) ** block_scale(key_list[3], (SEQS, MASK), ((0, 16),), -0.2, 0.2), 2.0, 10.0),
        "head": draw_head(jax.random.fold_in(key_list[7], 71), 0),
        "m_state": draw_m_state(jax.random.fold_in(key_list[7], 71), 0),
        "v_state": jnp.clip(jnp.exp(math.log(20.0) - 3.6888795 * jax.random.uniform(key_list[6], (SLABS, SLAB, D), jnp.float32) ** block_scale(key_list[6], (SLABS, SLAB, D), ((0, 2), (1, 16)), -0.2, 0.2)), 0.5, 20.0),
    }


BETA_ONE = 0.9
BETA_TWO = 0.999
ADAM_EPSILON = 1e-06
TRUST_EPSILON = 1e-06
LEARNING_RATE = 0.02

def reference(hidden, positions, labels, lse_rest, head, m_state, v_state):
    picked = jnp.take_along_axis(hidden, positions[:, :, None], axis=1).reshape(ROWS, D)
    head_copy = head.reshape(BLOCK, D).astype(jnp.bfloat16)
    scores = lax.dot_general(picked, head_copy, (((1,), (1,)), ((), ())), preferred_element_type=jnp.float32)
    rest_lse = lse_rest.reshape(ROWS)
    row_top = jnp.maximum(lax.optimization_barrier(jnp.max(scores, axis=1)), rest_lse)
    row_total = jnp.exp(rest_lse - row_top) + lax.optimization_barrier(jnp.sum(jnp.exp(scores - row_top[:, None]), axis=1))
    row_lse = row_top + jnp.log(row_total)
    label_flat = labels.reshape(ROWS)
    label_hits = label_flat[:, None] == jnp.arange(BLOCK, dtype=jnp.int32)[None, :]
    target = lax.optimization_barrier(jnp.sum(jnp.where(label_hits, scores, 0.0), axis=1))
    losses = (row_lse - target).reshape(SEQS, MASK)
    logit_grad = (jnp.exp(scores - row_lse[:, None]) - label_hits.astype(jnp.float32)).astype(jnp.bfloat16)
    head_grad = lax.dot_general(logit_grad, picked, (((0,), (0,)), ((), ())), preferred_element_type=jnp.float32)
    head_grad = head_grad.reshape(SLABS, SLAB, D)
    new_m = BETA_ONE * m_state + (1.0 - BETA_ONE) * head_grad
    new_v = BETA_TWO * v_state + (1.0 - BETA_TWO) * head_grad * head_grad
    first_fix = 1.0 - BETA_ONE ** STEP
    second_fix = 1.0 - BETA_TWO ** STEP
    update = new_m / first_fix / (jnp.sqrt(new_v / second_fix) + ADAM_EPSILON)
    weight_sq = lax.optimization_barrier(jnp.sum(head * head, axis=(1, 2)))
    update_sq = lax.optimization_barrier(jnp.sum(update * update, axis=(1, 2)))
    trust_ratio = jnp.sqrt(weight_sq) / (jnp.sqrt(update_sq) + TRUST_EPSILON)
    new_head = head - LEARNING_RATE * trust_ratio[:, None, None] * update
    return (losses, new_head, new_m, new_v)
```

```python
import functools

import jax
import jax.numpy as jnp
from jax import lax
from jax.experimental import pallas as pl
from jax.experimental.pallas import tpu as pltpu
from jax.sharding import PartitionSpec as P

STEP = 100
BETA_ONE = 0.9
BETA_TWO = 0.999
ADAM_EPSILON = 1e-06
TRUST_EPSILON = 1e-06
LEARNING_RATE = 0.02

MESH = pl.DeviceIdType.MESH
CORES = 2
INNER = 2
F32 = jnp.float32
BF16 = jnp.bfloat16


def step_kernel(
    n_dp,
    hidden_ref,
    positions_hbm,
    labels_hbm,
    lse_hbm,
    head_hbm,
    m_ref,
    v_ref,
    losses_ref,
    new_head_ref,
    new_m_ref,
    new_v_ref,
    tokens,
    picked,
    pieces,
    stage,
    rows16,
    score_own,
    score_other,
    grads,
    got_core,
    send_y,
    got_y,
    send_z,
    got_z,
    send_x,
    grad_x,
    state_far,
    m_buf,
    v_buf,
    positions_ref,
    labels_ref,
    lse_ref,
    head_ref,
    update_buf,
    sums_own,
    sums,
    load_sem,
    state_sem,
    all_sent,
    head_recv,
    outer_recv,
    inner_recv,
    core_recv,
    score_recv,
    rs_core_recv,
    rs_y_recv,
    rs_z_recv,
    x_recv,
    sum_recv,
    far_recv,
):
    n_outer = n_dp // (CORES * INNER)
    seqs, length, half = hidden_ref.shape
    masked = positions_ref.shape[1]
    own_rows = head_ref.shape[1]
    part = half // CORES
    dp = lax.axis_index("dp")
    v = lax.axis_index("vocab")
    c = lax.rem(dp, CORES)
    y = lax.rem(lax.div(dp, CORES), INNER)
    z = lax.div(dp, CORES * INNER)

    def at(z_to, y_to, c_to):
        return (z_to * INNER + y_to) * CORES + c_to

    def fwd(k):
        return lax.rem(z + k, n_outer)

    def back(k):
        return lax.rem(z + n_outer - k, n_outer)

    def near_last(n):
        return jnp.where(z < n_outer // 2, n_outer - n, n)

    def send(src, dst, ssem, rsem, dp_to, v_to):
        return pltpu.make_async_remote_copy(
            src_ref=src,
            dst_ref=dst,
            send_sem=ssem,
            recv_sem=rsem,
            device_id=(dp_to, v_to),
            device_id_type=MESH,
        )

    partner = at(z, y, 1 - c)
    other_y = at(z, 1 - y, c)

    def load(seq):
        return pltpu.make_async_copy(hidden_ref.at[seq], tokens.at[seq], load_sem.at[seq])

    load_positions = pltpu.make_async_copy(positions_hbm, positions_ref, state_sem.at[2])
    load_positions.start()
    load_head = pltpu.make_async_copy(head_hbm, head_ref, state_sem.at[5])
    load_head.start()
    for seq in range(seqs):
        load(seq).start()
    load_labels = pltpu.make_async_copy(labels_hbm, labels_ref, state_sem.at[3])
    load_lse = pltpu.make_async_copy(lse_hbm, lse_ref, state_sem.at[4])
    load_m = pltpu.make_async_copy(m_ref, m_buf, state_sem.at[0])
    load_v = pltpu.make_async_copy(v_ref, v_buf, state_sem.at[1])
    for copy in (load_labels, load_lse, load_m, load_v):
        copy.start()

    sent = []

    def finish():
        for low_k, high_k, copies in sent:

            @pl.loop(low_k, high_k)
            def _(k, copies=copies):
                for copy in copies(k):
                    copy.wait_send()

    barrier = pltpu.get_barrier_semaphore()

    def greet(dp_to, v_to):
        pl.semaphore_signal(barrier, inc=1, device_id=(dp_to, v_to), device_id_type=MESH)

    @pl.loop(1, n_outer)
    def _(k):
        greet(at(fwd(k), y, c), v)

    greet(other_y, v)
    greet(partner, v)
    greet(dp, 1 - v)
    greet(partner, 1 - v)
    def pick(seq):
        load(seq).wait()
        spots = positions_ref[pl.ds(seq, 1), :]
        hot = lax.broadcasted_iota(jnp.int32, (length, masked), 0) == spots
        picked[seq] = lax.dot_general(
            jnp.where(hot, 1.0, 0.0).astype(BF16),
            tokens[seq],
            (((0,), (0,)), ((), ())),
            preferred_element_type=F32,
        ).astype(BF16)

    def picks(low, high):
        @pl.loop(low, high)
        def _(seq):
            pick(seq)

    load_positions.wait()
    load_head.wait()
    pl.semaphore_wait(barrier, n_outer + 3)

    def head_part(v_of, c_of):
        start = pl.multiple_of(v_of * half + c_of * part, part)
        return head_ref.at[0, :, pl.ds(start, part)]

    slot = 2 * c + v
    head_copies = [
        send(head_part(v_to, c_to), pieces.at[slot], all_sent, head_recv.at[slot], at(z, y, c_to), v_to)
        for v_to, c_to in ((1 - v, c), (1 - v, 1 - c), (v, 1 - c))
    ]
    for copy in head_copies:
        copy.start()

    def state_cols(ref):
        return ref.at[0, :, pl.ds(pl.multiple_of((1 - v) * half, half), half)]

    state_copies = [
        send(state_cols(m_ref), state_far.at[0], all_sent, far_recv.at[0], dp, 1 - v),
        send(state_cols(v_ref), state_far.at[1], all_sent, far_recv.at[1], dp, 1 - v),
    ]
    sent.append((0, 1, lambda k: head_copies + state_copies))
    pieces[slot] = head_ref[0, :, pl.ds(pl.multiple_of(v * half + c * part, part), part)]
    whole_head = head_ref[0]
    weight_part = jnp.sum(whole_head * whole_head, axis=(0, 1), keepdims=True)

    picks(0, 1)
    for slot_from in (
        2 * (1 - c) + v,
        2 * c + 1 - v,
        2 * (1 - c) + 1 - v,
    ):
        send(
            head_part(0, 0), pieces.at[slot_from], all_sent, head_recv.at[slot_from], dp, 1 - v
        ).wait_recv()
    for k in range(2 * CORES):
        stage[k * own_rows : (k + 1) * own_rows, :] = pieces[k]
    columns = pl.ds(pl.multiple_of(c * part, part), part)
    rows16[z * INNER + y, :, columns] = stage[...].astype(BF16)
    columns_other = pl.ds(pl.multiple_of((1 - c) * part, part), part)

    def rows_of(z_of, y_of, cols):
        return rows16.at[z_of * INNER + y_of, :, cols]

    def outer_copy(k, z_of):
        ref = rows_of(z_of, y, columns)
        return send(ref, ref, all_sent, outer_recv.at[k], at(fwd(k), y, c), v)

    def inner_copy(k, y_of):
        ref = rows_of(back(k), y_of, columns)
        return send(ref, ref, all_sent, inner_recv.at[k], other_y, v)

    def core_copy(k, y_of, index, cols):
        ref = rows_of(back(k), y_of, cols)
        return send(ref, ref, all_sent, core_recv.at[index], partner, v)

    inner_copy(0, y).start()
    core_copy(0, y, 0, columns).start()
    sent.append((1, n_outer, lambda k: (outer_copy(k, z),)))
    sent.append(
        (
            0,
            n_outer,
            lambda k: (
                inner_copy(k, y),
                core_copy(k, y, k, columns),
                core_copy(k, 1 - y, n_outer + k, columns),
            ),
        )
    )

    @pl.loop(1, n_outer)
    def _(n):
        outer_copy(near_last(n), z).start()

    picks(1, seqs)

    @pl.loop(1, n_outer)
    def _(n):
        k = near_last(n)
        outer_copy(k, back(k)).wait_recv()
        inner_copy(k, y).start()
        core_copy(k, y, k, columns).start()

    load_labels.wait()
    load_lse.wait()

    inner_copy(0, 1 - y).wait_recv()
    core_copy(0, 1 - y, n_outer, columns).start()

    @pl.loop(1, n_outer)
    def _(n):
        k = near_last(n)
        inner_copy(k, 1 - y).wait_recv()
        core_copy(k, 1 - y, n_outer + k, columns).start()

    @pl.loop(0, n_outer)
    def _(k):
        core_copy(k, y, k, columns_other).wait_recv()

    @pl.loop(0, n_outer)
    def _(k):
        core_copy(k, 1 - y, n_outer + k, columns_other).wait_recv()

    block = n_dp * 2 * own_rows

    def score_copy(seq):
        return send(
            score_own.at[seq],
            score_other.at[seq],
            all_sent,
            score_recv.at[seq],
            dp,
            1 - v,
        )

    @pl.loop(0, seqs)
    def _(seq):
        score_own[seq] = lax.dot_general(
            picked[seq],
            rows16[...].reshape(block, half),
            (((1,), (1,)), ((), ())),
            preferred_element_type=F32,
        )
        score_copy(seq).start()

    sent.append((0, seqs, lambda seq: (score_copy(seq),)))
    grads[...] = jnp.zeros_like(grads)
    row = lax.broadcasted_iota(jnp.int32, (block, masked), 0)
    shift = own_rows.bit_length() - 1
    row_id = (
        (lax.shift_right_logical(row, shift) & 1) * (n_dp * own_rows)
        + lax.shift_right_logical(row, shift + 1) * own_rows
        + (row & (own_rows - 1))
    )

    @pl.loop(0, seqs)
    def _(seq):
        score_copy(seq).wait_recv()
        scores = jnp.transpose(score_own[seq] + score_other[seq])
        rest = lse_ref[pl.ds(seq, 1), :]
        top = jnp.maximum(jnp.max(scores, axis=0, keepdims=True), rest)
        total = jnp.exp(rest - top) + jnp.sum(jnp.exp(scores - top), axis=0, keepdims=True)
        row_lse = top + jnp.log(total)
        hits = row_id == labels_ref[pl.ds(seq, 1), :]
        target = jnp.sum(jnp.where(hits, scores, 0.0), axis=0, keepdims=True)
        losses_ref[pl.ds(seq, 1), :] = row_lse - target
        logit_grad = (jnp.exp(scores - row_lse) - jnp.where(hits, 1.0, 0.0)).astype(BF16)
        grads[...] += lax.dot_general(
            logit_grad, picked[seq], (((1,), (0,)), ((), ())), preferred_element_type=F32
        ).reshape(n_dp, 2 * own_rows, half)

    for copy in state_copies:
        copy.start()

    def rs_core(k, y_of):
        return send(
            grads.at[at(fwd(k), y_of, 1 - c)],
            got_core.at[k, y_of],
            all_sent,
            rs_core_recv.at[k, y_of],
            partner,
            v,
        )

    def rs_y(k):
        return send(send_y.at[k], got_y.at[k], all_sent, rs_y_recv.at[k], other_y, v)

    def rs_z(k):
        return send(
            send_z.at[k], got_z.at[k], all_sent, rs_z_recv.at[k], at(fwd(k), y, c), v
        )

    sent.append((0, n_outer, lambda k: (rs_core(k, 0), rs_core(k, 1), rs_y(k))))
    sent.append((1, n_outer, lambda k: (rs_z(k),)))

    def later(n):
        return lax.rem(near_last(n + 1), n_outer) * jnp.where(n == n_outer - 1, 0, 1)

    @pl.loop(0, n_outer)
    def _(n):
        rs_core(later(n), 1 - y).start()

    @pl.loop(0, n_outer)
    def _(n):
        rs_core(later(n), y).start()

    @pl.loop(0, n_outer)
    def _(n):
        k = later(n)
        rs_core(k, 1 - y).wait_recv()
        send_y[k] = grads[at(fwd(k), 1 - y, c)] + got_core[k, 1 - y]
        rs_y(k).start()

    @pl.loop(1, n_outer)
    def _(n):
        k = near_last(n)
        rs_core(k, y).wait_recv()
        rs_y(k).wait_recv()
        send_z[k] = grads[at(fwd(k), y, c)] + got_core[k, y] + got_y[k]
        rs_z(k).start()

    rs_core(0, y).wait_recv()
    rs_y(0).wait_recv()
    rows8 = grads[at(z, y, c)] + got_core[0, y] + got_y[0]
    for k in range(1, n_outer):
        rs_z(k).wait_recv()
        rows8 = rows8 + got_z[k]
    low, high = rows8[:own_rows], rows8[own_rows:]
    grad_near = jnp.where(v == 0, low, high)
    grad_far = jnp.where(v == 0, high, low)
    send_x[...] = grad_far
    x_copy = send(send_x, grad_x, all_sent, x_recv, dp, 1 - v)
    x_copy.start()
    sent.append((0, 1, lambda k: (x_copy,)))
    load_m.wait()
    load_v.wait()
    for copy in state_copies:
        copy.wait_recv()

    first_fix = 1.0 - BETA_ONE**STEP
    second_fix = 1.0 - BETA_TWO**STEP

    def lamb(grad, first, second):
        first = BETA_ONE * first + (1.0 - BETA_ONE) * grad
        second = BETA_TWO * second + (1.0 - BETA_TWO) * grad * grad
        update = first / first_fix / (jnp.sqrt(second / second_fix) + ADAM_EPSILON)
        return first, second, update

    def square_sum(values):
        return jnp.sum(values * values, axis=(0, 1), keepdims=True)

    def finish_half(grad, h):
        cols = pl.ds(pl.multiple_of(h * half, half), half)
        first, second, update = lamb(grad, m_buf[0, :, cols], v_buf[0, :, cols])
        new_m_ref[0, :, cols] = first
        new_v_ref[0, :, cols] = second
        update_buf[:, cols] = update
        return update

    lane = lax.broadcasted_iota(jnp.int32, (1, 128), 1)
    _, _, update_far = lamb(grad_far, state_far[0], state_far[1])
    sums_own[1] = jnp.where(lane == 0, square_sum(update_far), 0.0)
    near = jnp.where(
        lane == 0,
        square_sum(finish_half(grad_near, v)),
        jnp.where(lane == 1, weight_part, 0.0),
    )
    sums_own[0] = near

    def sum_far(to):
        return send(sums_own.at[1], sums.at[n_dp + dp], all_sent, sum_recv, to, 1 - v)

    def sum_near(to):
        return send(sums_own.at[0], sums.at[dp], all_sent, sum_recv, to, v)

    def to_dp(k):
        return lax.rem(dp + k, n_dp)

    sums[dp] = near

    @pl.loop(1, n_dp)
    def _(n):
        k = jnp.where(z < n_outer // 2, n_dp - n, n)
        sum_far(to_dp(k)).start()
        sum_near(to_dp(k)).start()

    sum_far(dp).start()

    sent.append((0, n_dp, lambda k: (sum_far(to_dp(k)),)))
    sent.append((1, n_dp, lambda k: (sum_near(to_dp(k)),)))
    x_copy.wait_recv()
    finish_half(grad_x[...], 1 - v)
    finish()
    arrivals = sums.at[pl.ds(0, 2 * n_dp - 1)]
    send(arrivals, arrivals, all_sent, sum_recv, dp, 1 - v).wait_recv()

    totals = jnp.sum(sums[...], axis=0)
    update_total = jnp.sum(jnp.where(lane == 0, totals, 0.0), axis=1, keepdims=True)
    weight_total = jnp.sum(jnp.where(lane == 1, totals, 0.0), axis=1, keepdims=True)
    trust = jnp.sqrt(weight_total) / (jnp.sqrt(update_total) + TRUST_EPSILON)
    new_head_ref[0] = head_ref[0] - LEARNING_RATE * trust * update_buf[...]


def store_kernel(*refs):
    count = (len(refs) - 1) // 2
    sems = refs[-1]
    copies = [
        pltpu.make_async_copy(refs[n], refs[count + n], sems.at[n]) for n in range(count)
    ]
    for copy in copies:
        copy.start()
    for copy in copies:
        copy.wait()


def fused_step(n_dp, hidden, positions, labels, lse_rest, head, m_state, v_state):
    seqs, length, half = hidden.shape
    masked = positions.shape[1]
    own_rows, width = head.shape[1], head.shape[2]
    n_outer = n_dp // (CORES * INNER)
    pair = 2 * own_rows
    part = half // CORES
    block = n_dp * pair
    vmem = pl.BlockSpec(memory_space=pltpu.VMEM)
    anywhere = pl.BlockSpec(memory_space=pltpu.HBM)
    dma = pltpu.SemaphoreType.DMA
    state = jax.ShapeDtypeStruct(head.shape, F32)
    operands = [
        pltpu.with_memory_space_constraint(operand, pltpu.HBM)
        for operand in (hidden, positions, labels, lse_rest, head, m_state, v_state)
    ]
    results = pl.pallas_call(
        functools.partial(step_kernel, n_dp),
        out_shape=(jax.ShapeDtypeStruct(lse_rest.shape, F32), state, state, state),
        in_specs=[anywhere] * 7,
        out_specs=(vmem, vmem, vmem, vmem),
        scratch_shapes=[
            pltpu.VMEM((seqs, length, half), BF16),
            pltpu.VMEM((seqs, masked, half), BF16),
            pltpu.VMEM((2 * CORES, own_rows, part), F32),
            pltpu.VMEM((2 * CORES * own_rows, part), F32),
            pltpu.VMEM((n_dp // CORES, CORES * pair, half), BF16),
            pltpu.VMEM((seqs, masked, block), F32),
            pltpu.VMEM((seqs, masked, block), F32),
            pltpu.VMEM((n_dp, pair, half), F32),
            pltpu.VMEM((n_outer, INNER, pair, half), F32),
            pltpu.VMEM((n_outer, pair, half), F32),
            pltpu.VMEM((n_outer, pair, half), F32),
            pltpu.VMEM((n_outer, pair, half), F32),
            pltpu.VMEM((n_outer, pair, half), F32),
            pltpu.VMEM((own_rows, half), F32),
            pltpu.VMEM((own_rows, half), F32),
            pltpu.VMEM((2, own_rows, half), F32),
            pltpu.VMEM((1, own_rows, width), F32),
            pltpu.VMEM((1, own_rows, width), F32),
            pltpu.VMEM(positions.shape, jnp.int32),
            pltpu.VMEM(labels.shape, jnp.int32),
            pltpu.VMEM(lse_rest.shape, F32),
            pltpu.VMEM(head.shape, F32),
            pltpu.VMEM((own_rows, width), F32),
            pltpu.VMEM((2, 1, 128), F32),
            pltpu.VMEM((2 * n_dp, 1, 128), F32),
            dma((seqs,)),
            dma((6,)),
            dma,
            dma((2 * CORES,)),
            dma((n_outer,)),
            dma((n_outer,)),
            dma((2 * n_outer,)),
            dma((seqs,)),
            dma((n_outer, INNER)),
            dma((n_outer,)),
            dma((n_outer,)),
            dma,
            dma,
            dma((2,)),
        ],
        compiler_params=pltpu.CompilerParams(
            collective_id=0, has_side_effects=True, vmem_limit_bytes=48 * 1024 * 1024
        ),
        name="fused_step",
    )(*operands)
    count = len(results)
    return pl.pallas_call(
        store_kernel,
        out_shape=tuple(jax.ShapeDtypeStruct(r.shape, r.dtype) for r in results),
        in_specs=[vmem] * count,
        out_specs=(anywhere,) * count,
        scratch_shapes=[dma((count,))],
        compiler_params=pltpu.CompilerParams(vmem_limit_bytes=4 * 1024 * 1024),
        name="store_results",
    )(*results)


def on_device(hidden, positions, labels, lse_rest, head, m_state, v_state):
    seq_here, mask_here = positions.shape
    rows_here = seq_here * mask_here
    own_rows = head.shape[1]
    model_width = head.shape[2]
    head_own = head.reshape(own_rows, model_width)
    weight_total = lax.psum(jnp.sum(head_own * head_own), "dp")
    local_rows = jnp.take_along_axis(hidden, positions[:, :, None], axis=1).reshape(
        rows_here, hidden.shape[2]
    )
    picked = lax.all_gather(local_rows, "vocab", axis=1, tiled=True)
    head_copy = head_own.astype(jnp.bfloat16)
    scores = lax.dot_general(
        picked,
        lax.all_gather(head_copy, "dp", axis=0, tiled=True),
        (((1,), (1,)), ((), ())),
        preferred_element_type=jnp.float32,
    )
    slab_width = scores.shape[1]
    offset = lax.axis_index("vocab") * slab_width
    label_local = labels.reshape(rows_here) - offset
    label_hits = label_local[:, None] == lax.iota(jnp.int32, slab_width)[None, :]
    target_part = jnp.sum(jnp.where(label_hits, scores, 0.0), axis=1)
    rest_lse = lse_rest.reshape(rows_here)
    slab_max = jnp.max(scores, axis=1)
    block_max = lax.pmax(slab_max, "vocab")
    row_top = jnp.maximum(block_max, rest_lse)
    slab_sum = jnp.sum(jnp.exp(scores - row_top[:, None]), axis=1)
    block_sum, target = lax.psum((slab_sum, target_part), "vocab")
    row_total = block_sum + jnp.exp(rest_lse - row_top)
    row_lse = row_top + jnp.log(row_total)
    losses = (row_lse - target).reshape(seq_here, mask_here)
    logit_grad = (jnp.exp(scores - row_lse[:, None]) - label_hits.astype(jnp.float32)).astype(
        jnp.bfloat16
    )
    full_grad = lax.dot_general(
        logit_grad, picked, (((0,), (0,)), ((), ())), preferred_element_type=jnp.float32
    )
    head_grad = lax.psum_scatter(full_grad, "dp", scatter_dimension=0, tiled=True)
    first_moment = BETA_ONE * m_state.reshape(own_rows, model_width) + (1.0 - BETA_ONE) * head_grad
    second_moment = (
        BETA_TWO * v_state.reshape(own_rows, model_width) + (1.0 - BETA_TWO) * head_grad * head_grad
    )
    first_fix = 1.0 - BETA_ONE**STEP
    second_fix = 1.0 - BETA_TWO**STEP
    update = first_moment / first_fix / (jnp.sqrt(second_moment / second_fix) + ADAM_EPSILON)
    update_part = jnp.sum(update * update)
    update_total = lax.psum(update_part, "dp")
    trust_ratio = jnp.sqrt(weight_total) / (jnp.sqrt(update_total) + TRUST_EPSILON)
    new_head = head_own - LEARNING_RATE * trust_ratio * update
    return (
        losses,
        new_head.reshape(head.shape),
        first_moment.reshape(head.shape),
        second_moment.reshape(head.shape),
    )


def pairwise(mesh, args):
    n_dp, n_vocab = mesh.shape["dp"], mesh.shape["vocab"]
    own_rows = args[4].shape[1] // n_dp
    power_of_two = own_rows & (own_rows - 1) == 0
    return n_vocab == 2 and n_dp % (CORES * INNER) == 0 and power_of_two


def solution(mesh):
    def step(*args):
        if pairwise(mesh, args):
            body = functools.partial(fused_step, mesh.shape["dp"])
        else:
            body = on_device
        return sharded(mesh, body)(*args)

    return step


def sharded(mesh, body):
    return jax.shard_map(
        body,
        mesh=mesh,
        in_specs=(
            P("dp", None, "vocab"),
            P("dp", None),
            P("dp", None),
            P("dp", None),
            P("vocab", "dp", None),
            P("vocab", "dp", None),
            P("vocab", "dp", None),
        ),
        out_specs=(
            P("dp", None),
            P("vocab", "dp", None),
            P("vocab", "dp", None),
            P("vocab", "dp", None),
        ),
        check_vma=False,
    )
```

```python
import functools

import jax
import jax.numpy as jnp
from jax import lax
from jax.experimental import pallas as pl
from jax.experimental.pallas import tpu as pltpu
from jax.sharding import PartitionSpec as P

STEP = 100
BETA_ONE = 0.9
BETA_TWO = 0.999
ADAM_EPSILON = 1e-06
TRUST_EPSILON = 1e-06
LEARNING_RATE = 0.02

MESH = pl.DeviceIdType.MESH
CORES = 2
INNER = 2
F32 = jnp.float32
BF16 = jnp.bfloat16


def step_kernel(
    n_dp,
    hidden_ref,
    positions_hbm,
    labels_hbm,
    lse_hbm,
    head_hbm,
    m_ref,
    v_ref,
    losses_ref,
    new_head_ref,
    new_m_ref,
    new_v_ref,
    tokens,
    picked,
    pieces,
    across,
    score_own,
    score_other,
    grads,
    got_core,
    send_y,
    got_y,
    send_z,
    got_z,
    send_x,
    grad_x,
    state_far,
    m_buf,
    v_buf,
    positions_ref,
    labels_ref,
    lse_ref,
    head_ref,
    update_buf,
    sums_own,
    sums,
    load_sem,
    state_sem,
    all_sent,
    x_head_recv,
    outer_recv,
    inner_recv,
    core_recv,
    score_recv,
    rs_core_recv,
    rs_y_recv,
    rs_z_recv,
    x_recv,
    sum_recv,
    far_recv,
):
    n_outer = n_dp // (CORES * INNER)
    seqs, length, half = hidden_ref.shape
    masked = positions_ref.shape[1]
    own_rows = head_ref.shape[1]
    dp = lax.axis_index("dp")
    v = lax.axis_index("vocab")
    c = lax.rem(dp, CORES)
    y = lax.rem(lax.div(dp, CORES), INNER)
    z = lax.div(dp, CORES * INNER)

    def at(z_to, y_to, c_to):
        return (z_to * INNER + y_to) * CORES + c_to

    def spot(z_of, y_of, c_of):
        return (y_of * CORES + c_of) * n_outer + z_of

    def fwd(k):
        return lax.rem(z + k, n_outer)

    def near_last(n):
        return jnp.where(z < n_outer // 2, n_outer - n, n)

    def send(src, dst, ssem, rsem, dp_to, v_to):
        return pltpu.make_async_remote_copy(
            src_ref=src,
            dst_ref=dst,
            send_sem=ssem,
            recv_sem=rsem,
            device_id=(dp_to, v_to),
            device_id_type=MESH,
        )

    partner = at(z, y, 1 - c)
    other_y = at(z, 1 - y, c)

    def load(seq):
        return pltpu.make_async_copy(hidden_ref.at[seq], tokens.at[seq], load_sem.at[seq])

    load_positions = pltpu.make_async_copy(positions_hbm, positions_ref, state_sem.at[2])
    load_positions.start()
    load_head = pltpu.make_async_copy(head_hbm, head_ref, state_sem.at[5])
    load_head.start()
    for seq in range(seqs):
        load(seq).start()
    load_labels = pltpu.make_async_copy(labels_hbm, labels_ref, state_sem.at[3])
    load_lse = pltpu.make_async_copy(lse_hbm, lse_ref, state_sem.at[4])
    load_m = pltpu.make_async_copy(m_ref, m_buf, state_sem.at[0])
    load_v = pltpu.make_async_copy(v_ref, v_buf, state_sem.at[1])
    for copy in (load_labels, load_lse, load_m, load_v):
        copy.start()

    sent = []

    def finish():
        for low_k, high_k, copies in sent:

            @pl.loop(low_k, high_k)
            def _(k, copies=copies):
                for copy in copies(k):
                    copy.wait_send()

    barrier = pltpu.get_barrier_semaphore()

    def greet(dp_to, v_to):
        pl.semaphore_signal(barrier, inc=1, device_id=(dp_to, v_to), device_id_type=MESH)

    @pl.loop(1, n_outer)
    def _(k):
        greet(at(fwd(k), y, c), v)

    greet(other_y, v)
    greet(partner, v)
    greet(dp, 1 - v)

    def pick(seq):
        load(seq).wait()
        spots = positions_ref[pl.ds(seq, 1), :]
        hot = lax.broadcasted_iota(jnp.int32, (length, masked), 0) == spots
        picked[seq] = lax.dot_general(
            jnp.where(hot, 1.0, 0.0).astype(BF16),
            tokens[seq],
            (((0,), (0,)), ((), ())),
            preferred_element_type=F32,
        ).astype(BF16)

    def picks(low, high):
        @pl.loop(low, high)
        def _(seq):
            pick(seq)

    load_head.wait()
    pl.semaphore_wait(barrier, n_outer + 2)

    def pair(z_of, y_of, c_of):
        return pieces.at[spot(z_of, y_of, c_of)]

    def piece(z_of, slab):
        return pair(z_of, y, c).at[slab]

    def half_of(h):
        return head_ref[0, :, pl.ds(pl.multiple_of(h * half, half), half)].astype(BF16)

    def x_head():
        return send(across, piece(z, v), all_sent, x_head_recv, dp, 1 - v)

    def outer_copy(z_to, slab):
        ref = piece(z, slab)
        return send(ref, ref, all_sent, outer_recv.at[z], at(z_to, y, c), v)

    def inner_copy(z_of):
        ref = pair(z_of, y, c)
        return send(ref, ref, all_sent, inner_recv.at[z_of], other_y, v)

    def core_copy(z_of, y_of):
        ref = pair(z_of, y_of, c)
        return send(ref, ref, all_sent, core_recv.at[y_of], partner, v)

    def others(d, step):
        for other in (z - d, z + d):

            @pl.when((other >= 0) & (other < n_outer))
            def _(other=other):
                step(other)

    def far_first(step):
        @pl.loop(1, n_outer)
        def _(n):
            others(n_outer - n, step)

    def near_first(step):
        @pl.loop(1, n_outer)
        def _(d):
            others(d, step)

    early, late = 2 * seqs // 5, 4 * seqs // 5
    across[...] = half_of(1 - v)
    pieces[spot(z, y, c), v] = half_of(v)
    x_head().start()
    far_first(lambda z_to: outer_copy(z_to, v).start())
    load_positions.wait()
    picks(0, early)
    whole_head = head_ref[0]
    weight_part = jnp.sum(whole_head * whole_head, axis=(0, 1), keepdims=True)
    send(across, piece(z, 1 - v), all_sent, x_head_recv, dp, 1 - v).wait_recv()
    far_first(lambda z_to: outer_copy(z_to, 1 - v).start())
    inner_copy(z).start()
    core_copy(z, y).start()
    picks(early, late)

    def pass_on(z_from):
        ref = pair(z_from, y, c)
        send(ref, ref, all_sent, outer_recv.at[z_from], dp, 1 - v).wait_recv()
        inner_copy(z_from).start()
        core_copy(z_from, y).start()

    near_first(pass_on)
    picks(late, seqs)
    load_labels.wait()
    load_lse.wait()

    def pass_core(z_from):
        ref = pair(z_from, 1 - y, c)
        send(ref, ref, all_sent, inner_recv.at[z_from], dp, 1 - v).wait_recv()
        core_copy(z_from, 1 - y).start()

    pass_core(z)
    near_first(pass_core)
    for y_of in (y, 1 - y):
        ref = pieces.at[pl.ds(spot(0, y_of, 1 - c), n_outer)]
        send(ref, ref, all_sent, core_recv.at[y_of], dp, 1 - v).wait_recv()

    def state_cols(ref):
        return ref.at[0, :, pl.ds(pl.multiple_of((1 - v) * half, half), half)]

    state_copies = [
        send(state_cols(m_ref), state_far.at[0], all_sent, far_recv.at[0], dp, 1 - v),
        send(state_cols(v_ref), state_far.at[1], all_sent, far_recv.at[1], dp, 1 - v),
    ]
    sent.append((0, 1, lambda k: state_copies + [x_head()]))
    sent.append((1, n_outer, lambda k: (outer_copy(z, 0), outer_copy(z, 1))))
    sent.append((0, n_outer, lambda k: (inner_copy(k), core_copy(k, 0), core_copy(k, 1))))

    block = n_dp * 2 * own_rows

    def score_copy(seq):
        return send(
            score_own.at[seq],
            score_other.at[seq],
            all_sent,
            score_recv.at[seq],
            dp,
            1 - v,
        )

    @pl.loop(0, seqs)
    def _(seq):
        score_own[seq] = lax.dot_general(
            picked[seq],
            pieces[...].reshape(block, half),
            (((1,), (1,)), ((), ())),
            preferred_element_type=F32,
        )
        score_copy(seq).start()

    sent.append((0, seqs, lambda seq: (score_copy(seq),)))
    grads[...] = jnp.zeros_like(grads)
    row = lax.broadcasted_iota(jnp.int32, (block, masked), 0)
    shift = own_rows.bit_length() - 1
    slot = lax.shift_right_logical(row, shift + 1)
    outer_bits = n_outer.bit_length() - 1
    slot_z = slot & (n_outer - 1)
    slot_c = lax.shift_right_logical(slot, outer_bits) & (CORES - 1)
    slot_y = lax.shift_right_logical(slot, outer_bits + CORES.bit_length() - 1)
    row_id = (
        (lax.shift_right_logical(row, shift) & 1) * (n_dp * own_rows)
        + at(slot_z, slot_y, slot_c) * own_rows
        + (row & (own_rows - 1))
    )

    @pl.loop(0, seqs)
    def _(seq):
        score_copy(seq).wait_recv()
        scores = jnp.transpose(score_own[seq] + score_other[seq])
        rest = lse_ref[pl.ds(seq, 1), :]
        top = jnp.maximum(jnp.max(scores, axis=0, keepdims=True), rest)
        total = jnp.exp(rest - top) + jnp.sum(jnp.exp(scores - top), axis=0, keepdims=True)
        row_lse = top + jnp.log(total)
        hits = row_id == labels_ref[pl.ds(seq, 1), :]
        target = jnp.sum(jnp.where(hits, scores, 0.0), axis=0, keepdims=True)
        losses_ref[pl.ds(seq, 1), :] = row_lse - target
        logit_grad = (jnp.exp(scores - row_lse) - jnp.where(hits, 1.0, 0.0)).astype(BF16)
        grads[...] += lax.dot_general(
            logit_grad, picked[seq], (((1,), (0,)), ((), ())), preferred_element_type=F32
        ).reshape(n_dp, 2 * own_rows, half)

    for copy in state_copies:
        copy.start()

    def rs_core(k, y_of):
        return send(
            grads.at[spot(fwd(k), y_of, 1 - c)],
            got_core.at[k, y_of],
            all_sent,
            rs_core_recv.at[k, y_of],
            partner,
            v,
        )

    def rs_y(k):
        return send(send_y.at[k], got_y.at[k], all_sent, rs_y_recv.at[k], other_y, v)

    def rs_z(k):
        return send(
            send_z.at[k], got_z.at[k], all_sent, rs_z_recv.at[k], at(fwd(k), y, c), v
        )

    sent.append((0, n_outer, lambda k: (rs_core(k, 0), rs_core(k, 1), rs_y(k))))
    sent.append((1, n_outer, lambda k: (rs_z(k),)))

    def later(n):
        return lax.rem(near_last(n + 1), n_outer) * jnp.where(n == n_outer - 1, 0, 1)

    @pl.loop(0, n_outer)
    def _(n):
        rs_core(later(n), 1 - y).start()

    @pl.loop(0, n_outer)
    def _(n):
        rs_core(later(n), y).start()

    @pl.loop(0, n_outer)
    def _(n):
        k = later(n)
        rs_core(k, 1 - y).wait_recv()
        send_y[k] = grads[spot(fwd(k), 1 - y, c)] + got_core[k, 1 - y]
        rs_y(k).start()

    @pl.loop(1, n_outer)
    def _(n):
        k = near_last(n)
        rs_core(k, y).wait_recv()
        rs_y(k).wait_recv()
        send_z[k] = grads[spot(fwd(k), y, c)] + got_core[k, y] + got_y[k]
        rs_z(k).start()

    rs_core(0, y).wait_recv()
    rs_y(0).wait_recv()
    rows8 = grads[spot(z, y, c)] + got_core[0, y] + got_y[0]
    for k in range(1, n_outer):
        rs_z(k).wait_recv()
        rows8 = rows8 + got_z[k]
    low, high = rows8[:own_rows], rows8[own_rows:]
    grad_near = jnp.where(v == 0, low, high)
    grad_far = jnp.where(v == 0, high, low)
    send_x[...] = grad_far
    x_copy = send(send_x, grad_x, all_sent, x_recv, dp, 1 - v)
    x_copy.start()
    sent.append((0, 1, lambda k: (x_copy,)))
    load_m.wait()
    load_v.wait()
    for copy in state_copies:
        copy.wait_recv()

    first_fix = 1.0 - BETA_ONE**STEP
    second_fix = 1.0 - BETA_TWO**STEP

    def lamb(grad, first, second):
        first = BETA_ONE * first + (1.0 - BETA_ONE) * grad
        second = BETA_TWO * second + (1.0 - BETA_TWO) * grad * grad
        update = first / first_fix / (jnp.sqrt(second / second_fix) + ADAM_EPSILON)
        return first, second, update

    def square_sum(values):
        return jnp.sum(values * values, axis=(0, 1), keepdims=True)

    def finish_half(grad, h):
        cols = pl.ds(pl.multiple_of(h * half, half), half)
        first, second, update = lamb(grad, m_buf[0, :, cols], v_buf[0, :, cols])
        new_m_ref[0, :, cols] = first
        new_v_ref[0, :, cols] = second
        update_buf[:, cols] = update
        return update

    lane = lax.broadcasted_iota(jnp.int32, (1, 128), 1)
    _, _, update_far = lamb(grad_far, state_far[0], state_far[1])
    sums_own[1] = jnp.where(lane == 0, square_sum(update_far), 0.0)
    near = jnp.where(
        lane == 0,
        square_sum(finish_half(grad_near, v)),
        jnp.where(lane == 1, weight_part, 0.0),
    )
    sums_own[0] = near

    def sum_far(to):
        return send(sums_own.at[1], sums.at[n_dp + dp], all_sent, sum_recv, to, 1 - v)

    def sum_near(to):
        return send(sums_own.at[0], sums.at[dp], all_sent, sum_recv, to, v)

    def to_dp(k):
        return lax.rem(dp + k, n_dp)

    sums[dp] = near

    @pl.loop(1, n_dp)
    def _(n):
        k = jnp.where(z < n_outer // 2, n_dp - n, n)
        sum_far(to_dp(k)).start()
        sum_near(to_dp(k)).start()

    sum_far(dp).start()

    sent.append((0, n_dp, lambda k: (sum_far(to_dp(k)),)))
    sent.append((1, n_dp, lambda k: (sum_near(to_dp(k)),)))
    x_copy.wait_recv()
    finish_half(grad_x[...], 1 - v)
    finish()
    arrivals = sums.at[pl.ds(0, 2 * n_dp - 1)]
    send(arrivals, arrivals, all_sent, sum_recv, dp, 1 - v).wait_recv()

    totals = jnp.sum(sums[...], axis=0)
    update_total = jnp.sum(jnp.where(lane == 0, totals, 0.0), axis=1, keepdims=True)
    weight_total = jnp.sum(jnp.where(lane == 1, totals, 0.0), axis=1, keepdims=True)
    trust = jnp.sqrt(weight_total) / (jnp.sqrt(update_total) + TRUST_EPSILON)
    new_head_ref[0] = head_ref[0] - LEARNING_RATE * trust * update_buf[...]


def store_kernel(*refs):
    count = (len(refs) - 1) // 2
    sems = refs[-1]
    copies = [
        pltpu.make_async_copy(refs[n], refs[count + n], sems.at[n]) for n in range(count)
    ]
    for copy in copies:
        copy.start()
    for copy in copies:
        copy.wait()


def fused_step(n_dp, hidden, positions, labels, lse_rest, head, m_state, v_state):
    seqs, length, half = hidden.shape
    masked = positions.shape[1]
    own_rows, width = head.shape[1], head.shape[2]
    n_outer = n_dp // (CORES * INNER)
    pair = 2 * own_rows
    block = n_dp * pair
    vmem = pl.BlockSpec(memory_space=pltpu.VMEM)
    anywhere = pl.BlockSpec(memory_space=pltpu.HBM)
    dma = pltpu.SemaphoreType.DMA
    state = jax.ShapeDtypeStruct(head.shape, F32)
    operands = [
        pltpu.with_memory_space_constraint(operand, pltpu.HBM)
        for operand in (hidden, positions, labels, lse_rest, head, m_state, v_state)
    ]
    results = pl.pallas_call(
        functools.partial(step_kernel, n_dp),
        out_shape=(jax.ShapeDtypeStruct(lse_rest.shape, F32), state, state, state),
        in_specs=[anywhere] * 7,
        out_specs=(vmem, vmem, vmem, vmem),
        scratch_shapes=[
            pltpu.VMEM((seqs, length, half), BF16),
            pltpu.VMEM((seqs, masked, half), BF16),
            pltpu.VMEM((n_dp, 2, own_rows, half), BF16),
            pltpu.VMEM((own_rows, half), BF16),
            pltpu.VMEM((seqs, masked, block), F32),
            pltpu.VMEM((seqs, masked, block), F32),
            pltpu.VMEM((n_dp, pair, half), F32),
            pltpu.VMEM((n_outer, INNER, pair, half), F32),
            pltpu.VMEM((n_outer, pair, half), F32),
            pltpu.VMEM((n_outer, pair, half), F32),
            pltpu.VMEM((n_outer, pair, half), F32),
            pltpu.VMEM((n_outer, pair, half), F32),
            pltpu.VMEM((own_rows, half), F32),
            pltpu.VMEM((own_rows, half), F32),
            pltpu.VMEM((2, own_rows, half), F32),
            pltpu.VMEM((1, own_rows, width), F32),
            pltpu.VMEM((1, own_rows, width), F32),
            pltpu.VMEM(positions.shape, jnp.int32),
            pltpu.VMEM(labels.shape, jnp.int32),
            pltpu.VMEM(lse_rest.shape, F32),
            pltpu.VMEM(head.shape, F32),
            pltpu.VMEM((own_rows, width), F32),
            pltpu.VMEM((2, 1, 128), F32),
            pltpu.VMEM((2 * n_dp, 1, 128), F32),
            dma((seqs,)),
            dma((6,)),
            dma,
            dma,
            dma((n_outer,)),
            dma((n_outer,)),
            dma((INNER,)),
            dma((seqs,)),
            dma((n_outer, INNER)),
            dma((n_outer,)),
            dma((n_outer,)),
            dma,
            dma,
            dma((2,)),
        ],
        compiler_params=pltpu.CompilerParams(
            collective_id=0, has_side_effects=True, vmem_limit_bytes=48 * 1024 * 1024
        ),
        name="fused_step",
    )(*operands)
    count = len(results)
    return pl.pallas_call(
        store_kernel,
        out_shape=tuple(jax.ShapeDtypeStruct(r.shape, r.dtype) for r in results),
        in_specs=[vmem] * count,
        out_specs=(anywhere,) * count,
        scratch_shapes=[dma((count,))],
        compiler_params=pltpu.CompilerParams(vmem_limit_bytes=4 * 1024 * 1024),
        name="store_results",
    )(*results)


def on_device(hidden, positions, labels, lse_rest, head, m_state, v_state):
    seq_here, mask_here = positions.shape
    rows_here = seq_here * mask_here
    own_rows = head.shape[1]
    model_width = head.shape[2]
    head_own = head.reshape(own_rows, model_width)
    weight_total = lax.psum(jnp.sum(head_own * head_own), "dp")
    local_rows = jnp.take_along_axis(hidden, positions[:, :, None], axis=1).reshape(
        rows_here, hidden.shape[2]
    )
    picked = lax.all_gather(local_rows, "vocab", axis=1, tiled=True)
    head_copy = head_own.astype(jnp.bfloat16)
    scores = lax.dot_general(
        picked,
        lax.all_gather(head_copy, "dp", axis=0, tiled=True),
        (((1,), (1,)), ((), ())),
        preferred_element_type=jnp.float32,
    )
    slab_width = scores.shape[1]
    offset = lax.axis_index("vocab") * slab_width
    label_local = labels.reshape(rows_here) - offset
    label_hits = label_local[:, None] == lax.iota(jnp.int32, slab_width)[None, :]
    target_part = jnp.sum(jnp.where(label_hits, scores, 0.0), axis=1)
    rest_lse = lse_rest.reshape(rows_here)
    slab_max = jnp.max(scores, axis=1)
    block_max = lax.pmax(slab_max, "vocab")
    row_top = jnp.maximum(block_max, rest_lse)
    slab_sum = jnp.sum(jnp.exp(scores - row_top[:, None]), axis=1)
    block_sum, target = lax.psum((slab_sum, target_part), "vocab")
    row_total = block_sum + jnp.exp(rest_lse - row_top)
    row_lse = row_top + jnp.log(row_total)
    losses = (row_lse - target).reshape(seq_here, mask_here)
    logit_grad = (jnp.exp(scores - row_lse[:, None]) - label_hits.astype(jnp.float32)).astype(
        jnp.bfloat16
    )
    full_grad = lax.dot_general(
        logit_grad, picked, (((0,), (0,)), ((), ())), preferred_element_type=jnp.float32
    )
    head_grad = lax.psum_scatter(full_grad, "dp", scatter_dimension=0, tiled=True)
    first_moment = BETA_ONE * m_state.reshape(own_rows, model_width) + (1.0 - BETA_ONE) * head_grad
    second_moment = (
        BETA_TWO * v_state.reshape(own_rows, model_width) + (1.0 - BETA_TWO) * head_grad * head_grad
    )
    first_fix = 1.0 - BETA_ONE**STEP
    second_fix = 1.0 - BETA_TWO**STEP
    update = first_moment / first_fix / (jnp.sqrt(second_moment / second_fix) + ADAM_EPSILON)
    update_part = jnp.sum(update * update)
    update_total = lax.psum(update_part, "dp")
    trust_ratio = jnp.sqrt(weight_total) / (jnp.sqrt(update_total) + TRUST_EPSILON)
    new_head = head_own - LEARNING_RATE * trust_ratio * update
    return (
        losses,
        new_head.reshape(head.shape),
        first_moment.reshape(head.shape),
        second_moment.reshape(head.shape),
    )


def pairwise(mesh, args):
    n_dp, n_vocab = mesh.shape["dp"], mesh.shape["vocab"]
    own_rows = args[4].shape[1] // n_dp
    power_of_two = own_rows & (own_rows - 1) == 0
    n_outer = n_dp // (CORES * INNER)
    power_of_two = power_of_two and n_outer & (n_outer - 1) == 0
    return n_vocab == 2 and n_dp % (CORES * INNER) == 0 and power_of_two


def solution(mesh):
    def step(*args):
        if pairwise(mesh, args):
            body = functools.partial(fused_step, mesh.shape["dp"])
        else:
            body = on_device
        return sharded(mesh, body)(*args)

    return step


def sharded(mesh, body):
    return jax.shard_map(
        body,
        mesh=mesh,
        in_specs=(
            P("dp", None, "vocab"),
            P("dp", None),
            P("dp", None),
            P("dp", None),
            P("vocab", "dp", None),
            P("vocab", "dp", None),
            P("vocab", "dp", None),
        ),
        out_specs=(
            P("dp", None),
            P("vocab", "dp", None),
            P("vocab", "dp", None),
            P("vocab", "dp", None),
        ),
        check_vma=False,
    )
```

```python
import functools

import jax
import jax.numpy as jnp
from jax import lax
from jax.experimental import pallas as pl
from jax.experimental.pallas import tpu as pltpu
from jax.sharding import PartitionSpec as P

STEP = 100
BETA_ONE = 0.9
BETA_TWO = 0.999
ADAM_EPSILON = 1e-06
TRUST_EPSILON = 1e-06
LEARNING_RATE = 0.02

MESH = pl.DeviceIdType.MESH
CORES = 2
INNER = 2
F32 = jnp.float32
BF16 = jnp.bfloat16


def step_kernel(
    n_dp,
    hidden_ref,
    positions_hbm,
    labels_hbm,
    lse_hbm,
    head_hbm,
    m_ref,
    v_ref,
    losses_ref,
    new_head_ref,
    new_m_ref,
    new_v_ref,
    tokens,
    picked,
    pieces,
    across,
    score_own,
    score_other,
    tail_own,
    tail_other,
    grads,
    got_core,
    send_y,
    got_y,
    send_z,
    got_z,
    send_x,
    grad_x,
    state_far,
    m_buf,
    v_buf,
    positions_ref,
    labels_ref,
    lse_ref,
    head_ref,
    update_buf,
    sums_own,
    sums,
    load_sem,
    state_sem,
    all_sent,
    x_head_recv,
    outer_recv,
    inner_recv,
    core_recv,
    score_recv,
    tail_recv,
    rs_core_recv,
    rs_y_recv,
    rs_z_recv,
    x_recv,
    sum_recv,
    far_recv,
):
    n_outer = n_dp // (CORES * INNER)
    seqs, length, half = hidden_ref.shape
    masked = positions_ref.shape[1]
    own_rows = head_ref.shape[1]
    dp = lax.axis_index("dp")
    v = lax.axis_index("vocab")
    c = lax.rem(dp, CORES)
    y = lax.rem(lax.div(dp, CORES), INNER)
    z = lax.div(dp, CORES * INNER)

    def at(z_to, y_to, c_to):
        return (z_to * INNER + y_to) * CORES + c_to

    def spot(z_of, y_of, c_of):
        return (y_of * CORES + c_of) * n_outer + z_of

    def fwd(k):
        return lax.rem(z + k, n_outer)

    def near_last(n):
        return jnp.where(z < n_outer // 2, n_outer - n, n)

    def send(src, dst, ssem, rsem, dp_to, v_to):
        return pltpu.make_async_remote_copy(
            src_ref=src,
            dst_ref=dst,
            send_sem=ssem,
            recv_sem=rsem,
            device_id=(dp_to, v_to),
            device_id_type=MESH,
        )

    partner = at(z, y, 1 - c)
    other_y = at(z, 1 - y, c)

    def load(seq):
        return pltpu.make_async_copy(hidden_ref.at[seq], tokens.at[seq], load_sem.at[seq])

    load_positions = pltpu.make_async_copy(positions_hbm, positions_ref, state_sem.at[2])
    load_positions.start()
    load_head = pltpu.make_async_copy(head_hbm, head_ref, state_sem.at[5])
    load_head.start()
    for seq in range(seqs):
        load(seq).start()
    load_labels = pltpu.make_async_copy(labels_hbm, labels_ref, state_sem.at[3])
    load_lse = pltpu.make_async_copy(lse_hbm, lse_ref, state_sem.at[4])
    load_m = pltpu.make_async_copy(m_ref, m_buf, state_sem.at[0])
    load_v = pltpu.make_async_copy(v_ref, v_buf, state_sem.at[1])
    for copy in (load_labels, load_lse, load_m, load_v):
        copy.start()

    sent = []

    def finish():
        for low_k, high_k, copies in sent:

            @pl.loop(low_k, high_k)
            def _(k, copies=copies):
                for copy in copies(k):
                    copy.wait_send()

    barrier = pltpu.get_barrier_semaphore()

    def greet(dp_to, v_to):
        pl.semaphore_signal(barrier, inc=1, device_id=(dp_to, v_to), device_id_type=MESH)

    @pl.loop(1, n_outer)
    def _(k):
        greet(at(fwd(k), y, c), v)

    greet(other_y, v)
    greet(partner, v)
    greet(dp, 1 - v)

    def pick(seq):
        load(seq).wait()
        spots = positions_ref[pl.ds(seq, 1), :]
        hot = lax.broadcasted_iota(jnp.int32, (length, masked), 0) == spots
        picked[seq] = lax.dot_general(
            jnp.where(hot, 1.0, 0.0).astype(BF16),
            tokens[seq],
            (((0,), (0,)), ((), ())),
            preferred_element_type=F32,
        ).astype(BF16)

    def picks(low, high):
        @pl.loop(low, high)
        def _(seq):
            pick(seq)

    load_head.wait()
    pl.semaphore_wait(barrier, n_outer + 2)

    def pair(z_of, y_of, c_of):
        return pieces.at[spot(z_of, y_of, c_of)]

    def piece(z_of, slab):
        return pair(z_of, y, c).at[slab]

    def half_of(h):
        return head_ref[0, :, pl.ds(pl.multiple_of(h * half, half), half)].astype(BF16)

    def x_head():
        return send(across, piece(z, v), all_sent, x_head_recv, dp, 1 - v)

    def outer_copy(z_to, slab):
        ref = piece(z, slab)
        return send(ref, ref, all_sent, outer_recv.at[z], at(z_to, y, c), v)

    def inner_copy(z_of):
        ref = pair(z_of, y, c)
        return send(ref, ref, all_sent, inner_recv.at[z_of], other_y, v)

    def core_copy(z_of, y_of):
        ref = pair(z_of, y_of, c)
        return send(ref, ref, all_sent, core_recv.at[y_of], partner, v)

    def others(d, step):
        for other in (z - d, z + d):

            @pl.when((other >= 0) & (other < n_outer))
            def _(other=other):
                step(other)

    def far_first(step):
        @pl.loop(1, n_outer)
        def _(n):
            others(n_outer - n, step)

    def near_first(step):
        @pl.loop(1, n_outer)
        def _(d):
            others(d, step)

    early, late = 2 * seqs // 5, 4 * seqs // 5
    across[...] = half_of(1 - v)
    pieces[spot(z, y, c), v] = half_of(v)
    x_head().start()
    far_first(lambda z_to: outer_copy(z_to, v).start())
    load_positions.wait()
    picks(0, early)
    whole_head = head_ref[0]
    weight_part = jnp.sum(whole_head * whole_head, axis=(0, 1), keepdims=True)
    send(across, piece(z, 1 - v), all_sent, x_head_recv, dp, 1 - v).wait_recv()
    far_first(lambda z_to: outer_copy(z_to, 1 - v).start())
    inner_copy(z).start()
    core_copy(z, y).start()
    picks(early, late)

    def pass_on(z_from):
        ref = pair(z_from, y, c)
        send(ref, ref, all_sent, outer_recv.at[z_from], dp, 1 - v).wait_recv()
        inner_copy(z_from).start()
        core_copy(z_from, y).start()

    near_first(pass_on)
    picks(late, seqs)
    load_labels.wait()
    load_lse.wait()

    def pass_core(z_from):
        ref = pair(z_from, 1 - y, c)
        send(ref, ref, all_sent, inner_recv.at[z_from], dp, 1 - v).wait_recv()
        core_copy(z_from, 1 - y).start()

    def core_wait(y_of):
        ref = pieces.at[pl.ds(spot(0, y_of, 1 - c), n_outer)]
        send(ref, ref, all_sent, core_recv.at[y_of], dp, 1 - v).wait_recv()

    block = n_dp * 2 * own_rows
    side = block // INNER
    pairs, odd = seqs // 2, seqs % 2
    cut = masked // 2

    def score_part(y_of, seq, count):
        near = pieces[pl.ds(y_of * (n_dp // INNER), n_dp // INNER)].reshape(side, half)
        return lax.dot_general(
            picked[pl.ds(seq, count)].reshape(count * masked, half),
            near,
            (((1,), (1,)), ((), ())),
            preferred_element_type=F32,
        )

    def score_copy(y_of, m):
        return send(
            score_own.at[y_of, m],
            score_other.at[y_of, m],
            all_sent,
            score_recv.at[y_of, m],
            dp,
            1 - v,
        )

    def tail_copy(y_of):
        return send(tail_own.at[y_of], tail_other.at[y_of], all_sent, tail_recv.at[y_of], dp, 1 - v)

    def send_pair(y_of, m):
        both = score_part(y_of, 2 * m, 2)
        score_own[y_of, m] = jnp.concatenate([both[:masked], both[masked:]], axis=1)
        score_copy(y_of, m).start()

    def send_tail(y_of):
        last = score_part(y_of, seqs - 1, 1)
        tail_own[y_of] = jnp.concatenate([last[:cut], last[cut:]], axis=1)
        tail_copy(y_of).start()

    tasks = [functools.partial(send_pair, y, m) for m in range(pairs)]
    if odd:
        tasks.append(functools.partial(send_tail, y))
    pass_core(z)
    core_wait(y)
    for d in range(1, n_outer):
        if tasks:
            tasks.pop(0)()
        others(d, pass_core)
    for task in tasks:
        task()
    core_wait(1 - y)

    @pl.loop(0, pairs)
    def _(m):
        send_pair(1 - y, m)

    if odd:
        send_tail(1 - y)
        sent.append((0, INNER, lambda k: (tail_copy(k),)))
    sent.append((0, pairs, lambda m: (score_copy(0, m), score_copy(1, m))))

    def state_cols(ref):
        return ref.at[0, :, pl.ds(pl.multiple_of((1 - v) * half, half), half)]

    state_copies = [
        send(state_cols(m_ref), state_far.at[0], all_sent, far_recv.at[0], dp, 1 - v),
        send(state_cols(v_ref), state_far.at[1], all_sent, far_recv.at[1], dp, 1 - v),
    ]
    sent.append((0, 1, lambda k: state_copies + [x_head()]))
    sent.append((1, n_outer, lambda k: (outer_copy(z, 0), outer_copy(z, 1))))
    sent.append((0, n_outer, lambda k: (inner_copy(k), core_copy(k, 0), core_copy(k, 1))))

    grads[...] = jnp.zeros_like(grads)
    row = lax.broadcasted_iota(jnp.int32, (block, masked), 0)
    shift = own_rows.bit_length() - 1
    slot = lax.shift_right_logical(row, shift + 1)
    outer_bits = n_outer.bit_length() - 1
    slot_z = slot & (n_outer - 1)
    slot_c = lax.shift_right_logical(slot, outer_bits) & (CORES - 1)
    slot_y = lax.shift_right_logical(slot, outer_bits + CORES.bit_length() - 1)
    row_id = (
        (lax.shift_right_logical(row, shift) & 1) * (n_dp * own_rows)
        + at(slot_z, slot_y, slot_c) * own_rows
        + (row & (own_rows - 1))
    )

    def finish_seq(seq, scores):
        rest = lse_ref[pl.ds(seq, 1), :]
        top = jnp.maximum(jnp.max(scores, axis=0, keepdims=True), rest)
        total = jnp.exp(rest - top) + jnp.sum(jnp.exp(scores - top), axis=0, keepdims=True)
        row_lse = top + jnp.log(total)
        hits = row_id == labels_ref[pl.ds(seq, 1), :]
        target = jnp.sum(jnp.where(hits, scores, 0.0), axis=0, keepdims=True)
        losses_ref[pl.ds(seq, 1), :] = row_lse - target
        logit_grad = (jnp.exp(scores - row_lse) - jnp.where(hits, 1.0, 0.0)).astype(BF16)
        grads[...] += lax.dot_general(
            logit_grad, picked[seq], (((1,), (0,)), ((), ())), preferred_element_type=F32
        ).reshape(n_dp, 2 * own_rows, half)

    @pl.loop(0, pairs)
    def _(m):
        turned = []
        for y_of in range(INNER):
            score_copy(y_of, m).wait_recv()
            turned.append(jnp.transpose(score_own[y_of, m] + score_other[y_of, m]))
        for n in range(2):
            rows = slice(n * side, (n + 1) * side)
            finish_seq(2 * m + n, jnp.concatenate([t[rows] for t in turned], axis=0))

    if odd:
        turned = []
        for y_of in range(INNER):
            tail_copy(y_of).wait_recv()
            turned.append(jnp.transpose(tail_own[y_of] + tail_other[y_of]))
        sides = [jnp.concatenate([t[n * side : (n + 1) * side] for t in turned], axis=0) for n in range(2)]
        finish_seq(seqs - 1, jnp.concatenate(sides, axis=1))

    for copy in state_copies:
        copy.start()

    def rs_core(k, y_of):
        return send(
            grads.at[spot(fwd(k), y_of, 1 - c)],
            got_core.at[k, y_of],
            all_sent,
            rs_core_recv.at[k, y_of],
            partner,
            v,
        )

    def rs_y(k):
        return send(send_y.at[k], got_y.at[k], all_sent, rs_y_recv.at[k], other_y, v)

    def rs_z(k):
        return send(
            send_z.at[k], got_z.at[k], all_sent, rs_z_recv.at[k], at(fwd(k), y, c), v
        )

    sent.append((0, n_outer, lambda k: (rs_core(k, 0), rs_core(k, 1), rs_y(k))))
    sent.append((1, n_outer, lambda k: (rs_z(k),)))

    def later(n):
        return lax.rem(near_last(n + 1), n_outer) * jnp.where(n == n_outer - 1, 0, 1)

    @pl.loop(0, n_outer)
    def _(n):
        rs_core(later(n), 1 - y).start()

    @pl.loop(0, n_outer)
    def _(n):
        rs_core(later(n), y).start()

    @pl.loop(0, n_outer)
    def _(n):
        k = later(n)
        rs_core(k, 1 - y).wait_recv()
        send_y[k] = grads[spot(fwd(k), 1 - y, c)] + got_core[k, 1 - y]
        rs_y(k).start()

    @pl.loop(1, n_outer)
    def _(n):
        k = near_last(n)
        rs_core(k, y).wait_recv()
        rs_y(k).wait_recv()
        send_z[k] = grads[spot(fwd(k), y, c)] + got_core[k, y] + got_y[k]
        rs_z(k).start()

    rs_core(0, y).wait_recv()
    rs_y(0).wait_recv()
    rows8 = grads[spot(z, y, c)] + got_core[0, y] + got_y[0]
    for k in range(1, n_outer):
        rs_z(k).wait_recv()
        rows8 = rows8 + got_z[k]
    low, high = rows8[:own_rows], rows8[own_rows:]
    grad_near = jnp.where(v == 0, low, high)
    grad_far = jnp.where(v == 0, high, low)
    send_x[...] = grad_far
    x_copy = send(send_x, grad_x, all_sent, x_recv, dp, 1 - v)
    x_copy.start()
    sent.append((0, 1, lambda k: (x_copy,)))
    load_m.wait()
    load_v.wait()
    for copy in state_copies:
        copy.wait_recv()

    first_fix = 1.0 - BETA_ONE**STEP
    second_fix = 1.0 - BETA_TWO**STEP

    def lamb(grad, first, second):
        first = BETA_ONE * first + (1.0 - BETA_ONE) * grad
        second = BETA_TWO * second + (1.0 - BETA_TWO) * grad * grad
        update = first / first_fix / (jnp.sqrt(second / second_fix) + ADAM_EPSILON)
        return first, second, update

    def square_sum(values):
        return jnp.sum(values * values, axis=(0, 1), keepdims=True)

    def finish_half(grad, h):
        cols = pl.ds(pl.multiple_of(h * half, half), half)
        first, second, update = lamb(grad, m_buf[0, :, cols], v_buf[0, :, cols])
        new_m_ref[0, :, cols] = first
        new_v_ref[0, :, cols] = second
        update_buf[:, cols] = update
        return update

    lane = lax.broadcasted_iota(jnp.int32, (1, 128), 1)
    _, _, update_far = lamb(grad_far, state_far[0], state_far[1])
    sums_own[1] = jnp.where(lane == 0, square_sum(update_far), 0.0)
    near = jnp.where(
        lane == 0,
        square_sum(finish_half(grad_near, v)),
        jnp.where(lane == 1, weight_part, 0.0),
    )
    sums_own[0] = near

    def sum_far(to):
        return send(sums_own.at[1], sums.at[n_dp + dp], all_sent, sum_recv, to, 1 - v)

    def sum_near(to):
        return send(sums_own.at[0], sums.at[dp], all_sent, sum_recv, to, v)

    def to_dp(k):
        return lax.rem(dp + k, n_dp)

    sums[dp] = near

    @pl.loop(1, n_dp)
    def _(n):
        k = jnp.where(z < n_outer // 2, n_dp - n, n)
        sum_far(to_dp(k)).start()
        sum_near(to_dp(k)).start()

    sum_far(dp).start()

    sent.append((0, n_dp, lambda k: (sum_far(to_dp(k)),)))
    sent.append((1, n_dp, lambda k: (sum_near(to_dp(k)),)))
    x_copy.wait_recv()
    finish_half(grad_x[...], 1 - v)
    finish()
    arrivals = sums.at[pl.ds(0, 2 * n_dp - 1)]
    send(arrivals, arrivals, all_sent, sum_recv, dp, 1 - v).wait_recv()

    totals = jnp.sum(sums[...], axis=0)
    update_total = jnp.sum(jnp.where(lane == 0, totals, 0.0), axis=1, keepdims=True)
    weight_total = jnp.sum(jnp.where(lane == 1, totals, 0.0), axis=1, keepdims=True)
    trust = jnp.sqrt(weight_total) / (jnp.sqrt(update_total) + TRUST_EPSILON)
    new_head_ref[0] = head_ref[0] - LEARNING_RATE * trust * update_buf[...]


def store_kernel(*refs):
    count = (len(refs) - 1) // 2
    sems = refs[-1]
    copies = [
        pltpu.make_async_copy(refs[n], refs[count + n], sems.at[n]) for n in range(count)
    ]
    for copy in copies:
        copy.start()
    for copy in copies:
        copy.wait()


def fused_step(n_dp, hidden, positions, labels, lse_rest, head, m_state, v_state):
    seqs, length, half = hidden.shape
    masked = positions.shape[1]
    own_rows, width = head.shape[1], head.shape[2]
    n_outer = n_dp // (CORES * INNER)
    pair = 2 * own_rows
    block = n_dp * pair
    vmem = pl.BlockSpec(memory_space=pltpu.VMEM)
    anywhere = pl.BlockSpec(memory_space=pltpu.HBM)
    dma = pltpu.SemaphoreType.DMA
    state = jax.ShapeDtypeStruct(head.shape, F32)
    operands = [
        pltpu.with_memory_space_constraint(operand, pltpu.HBM)
        for operand in (hidden, positions, labels, lse_rest, head, m_state, v_state)
    ]
    results = pl.pallas_call(
        functools.partial(step_kernel, n_dp),
        out_shape=(jax.ShapeDtypeStruct(lse_rest.shape, F32), state, state, state),
        in_specs=[anywhere] * 7,
        out_specs=(vmem, vmem, vmem, vmem),
        scratch_shapes=[
            pltpu.VMEM((seqs, length, half), BF16),
            pltpu.VMEM((seqs, masked, half), BF16),
            pltpu.VMEM((n_dp, 2, own_rows, half), BF16),
            pltpu.VMEM((own_rows, half), BF16),
            pltpu.VMEM((INNER, max(seqs // 2, 1), masked, block), F32),
            pltpu.VMEM((INNER, max(seqs // 2, 1), masked, block), F32),
            pltpu.VMEM((INNER, masked // 2, block), F32),
            pltpu.VMEM((INNER, masked // 2, block), F32),
            pltpu.VMEM((n_dp, pair, half), F32),
            pltpu.VMEM((n_outer, INNER, pair, half), F32),
            pltpu.VMEM((n_outer, pair, half), F32),
            pltpu.VMEM((n_outer, pair, half), F32),
            pltpu.VMEM((n_outer, pair, half), F32),
            pltpu.VMEM((n_outer, pair, half), F32),
            pltpu.VMEM((own_rows, half), F32),
            pltpu.VMEM((own_rows, half), F32),
            pltpu.VMEM((2, own_rows, half), F32),
            pltpu.VMEM((1, own_rows, width), F32),
            pltpu.VMEM((1, own_rows, width), F32),
            pltpu.VMEM(positions.shape, jnp.int32),
            pltpu.VMEM(labels.shape, jnp.int32),
            pltpu.VMEM(lse_rest.shape, F32),
            pltpu.VMEM(head.shape, F32),
            pltpu.VMEM((own_rows, width), F32),
            pltpu.VMEM((2, 1, 128), F32),
            pltpu.VMEM((2 * n_dp, 1, 128), F32),
            dma((seqs,)),
            dma((6,)),
            dma,
            dma,
            dma((n_outer,)),
            dma((n_outer,)),
            dma((INNER,)),
            dma((INNER, max(seqs // 2, 1))),
            dma((INNER,)),
            dma((n_outer, INNER)),
            dma((n_outer,)),
            dma((n_outer,)),
            dma,
            dma,
            dma((2,)),
        ],
        compiler_params=pltpu.CompilerParams(
            collective_id=0, has_side_effects=True, vmem_limit_bytes=48 * 1024 * 1024
        ),
        name="fused_step",
    )(*operands)
    count = len(results)
    return pl.pallas_call(
        store_kernel,
        out_shape=tuple(jax.ShapeDtypeStruct(r.shape, r.dtype) for r in results),
        in_specs=[vmem] * count,
        out_specs=(anywhere,) * count,
        scratch_shapes=[dma((count,))],
        compiler_params=pltpu.CompilerParams(vmem_limit_bytes=4 * 1024 * 1024),
        name="store_results",
    )(*results)


def on_device(hidden, positions, labels, lse_rest, head, m_state, v_state):
    seq_here, mask_here = positions.shape
    rows_here = seq_here * mask_here
    own_rows = head.shape[1]
    model_width = head.shape[2]
    head_own = head.reshape(own_rows, model_width)
    weight_total = lax.psum(jnp.sum(head_own * head_own), "dp")
    local_rows = jnp.take_along_axis(hidden, positions[:, :, None], axis=1).reshape(
        rows_here, hidden.shape[2]
    )
    picked = lax.all_gather(local_rows, "vocab", axis=1, tiled=True)
    head_copy = head_own.astype(jnp.bfloat16)
    scores = lax.dot_general(
        picked,
        lax.all_gather(head_copy, "dp", axis=0, tiled=True),
        (((1,), (1,)), ((), ())),
        preferred_element_type=jnp.float32,
    )
    slab_width = scores.shape[1]
    offset = lax.axis_index("vocab") * slab_width
    label_local = labels.reshape(rows_here) - offset
    label_hits = label_local[:, None] == lax.iota(jnp.int32, slab_width)[None, :]
    target_part = jnp.sum(jnp.where(label_hits, scores, 0.0), axis=1)
    rest_lse = lse_rest.reshape(rows_here)
    slab_max = jnp.max(scores, axis=1)
    block_max = lax.pmax(slab_max, "vocab")
    row_top = jnp.maximum(block_max, rest_lse)
    slab_sum = jnp.sum(jnp.exp(scores - row_top[:, None]), axis=1)
    block_sum, target = lax.psum((slab_sum, target_part), "vocab")
    row_total = block_sum + jnp.exp(rest_lse - row_top)
    row_lse = row_top + jnp.log(row_total)
    losses = (row_lse - target).reshape(seq_here, mask_here)
    logit_grad = (jnp.exp(scores - row_lse[:, None]) - label_hits.astype(jnp.float32)).astype(
        jnp.bfloat16
    )
    full_grad = lax.dot_general(
        logit_grad, picked, (((0,), (0,)), ((), ())), preferred_element_type=jnp.float32
    )
    head_grad = lax.psum_scatter(full_grad, "dp", scatter_dimension=0, tiled=True)
    first_moment = BETA_ONE * m_state.reshape(own_rows, model_width) + (1.0 - BETA_ONE) * head_grad
    second_moment = (
        BETA_TWO * v_state.reshape(own_rows, model_width) + (1.0 - BETA_TWO) * head_grad * head_grad
    )
    first_fix = 1.0 - BETA_ONE**STEP
    second_fix = 1.0 - BETA_TWO**STEP
    update = first_moment / first_fix / (jnp.sqrt(second_moment / second_fix) + ADAM_EPSILON)
    update_part = jnp.sum(update * update)
    update_total = lax.psum(update_part, "dp")
    trust_ratio = jnp.sqrt(weight_total) / (jnp.sqrt(update_total) + TRUST_EPSILON)
    new_head = head_own - LEARNING_RATE * trust_ratio * update
    return (
        losses,
        new_head.reshape(head.shape),
        first_moment.reshape(head.shape),
        second_moment.reshape(head.shape),
    )


def pairwise(mesh, args):
    n_dp, n_vocab = mesh.shape["dp"], mesh.shape["vocab"]
    own_rows = args[4].shape[1] // n_dp
    power_of_two = own_rows & (own_rows - 1) == 0
    n_outer = n_dp // (CORES * INNER)
    power_of_two = power_of_two and n_outer & (n_outer - 1) == 0
    masked = args[1].shape[1]
    power_of_two = power_of_two and masked % 16 == 0
    return n_vocab == 2 and n_dp % (CORES * INNER) == 0 and power_of_two


def solution(mesh):
    def step(*args):
        if pairwise(mesh, args):
            body = functools.partial(fused_step, mesh.shape["dp"])
        else:
            body = on_device
        return sharded(mesh, body)(*args)

    return step


def sharded(mesh, body):
    return jax.shard_map(
        body,
        mesh=mesh,
        in_specs=(
            P("dp", None, "vocab"),
            P("dp", None),
            P("dp", None),
            P("dp", None),
            P("vocab", "dp", None),
            P("vocab", "dp", None),
            P("vocab", "dp", None),
        ),
        out_specs=(
            P("dp", None),
            P("vocab", "dp", None),
            P("vocab", "dp", None),
            P("vocab", "dp", None),
        ),
        check_vma=False,
    )
```

```python
import functools

import jax
import jax.numpy as jnp
from jax import lax
from jax.experimental import pallas as pl
from jax.experimental.pallas import tpu as pltpu
from jax.sharding import PartitionSpec as P

STEP = 100
BETA_ONE = 0.9
BETA_TWO = 0.999
ADAM_EPSILON = 1e-06
TRUST_EPSILON = 1e-06
LEARNING_RATE = 0.02

MESH = pl.DeviceIdType.MESH
CORES = 2
INNER = 2
F32 = jnp.float32
BF16 = jnp.bfloat16


def step_kernel(
    n_dp,
    hidden_ref,
    positions_hbm,
    labels_hbm,
    lse_hbm,
    head_hbm,
    m_ref,
    v_ref,
    losses_ref,
    new_head_ref,
    new_m_ref,
    new_v_ref,
    tokens,
    picked,
    pieces,
    across,
    score_own,
    score_other,
    tail_own,
    tail_other,
    grads,
    got_core,
    send_y,
    got_y,
    send_z,
    got_z,
    send_x,
    grad_x,
    state_far,
    m_buf,
    v_buf,
    positions_ref,
    labels_ref,
    lse_ref,
    head_ref,
    update_buf,
    sums_own,
    sums,
    load_sem,
    state_sem,
    all_sent,
    x_head_recv,
    outer_recv,
    inner_recv,
    core_recv,
    score_recv,
    tail_recv,
    rs_core_recv,
    rs_y_recv,
    rs_z_recv,
    x_recv,
    sum_recv,
    far_recv,
):
    n_outer = n_dp // (CORES * INNER)
    seqs, length, half = hidden_ref.shape
    masked = positions_ref.shape[1]
    own_rows = head_ref.shape[1]
    dp = lax.axis_index("dp")
    v = lax.axis_index("vocab")
    c = lax.rem(dp, CORES)
    y = lax.rem(lax.div(dp, CORES), INNER)
    z = lax.div(dp, CORES * INNER)

    def at(z_to, y_to, c_to):
        return (z_to * INNER + y_to) * CORES + c_to

    def spot(z_of, y_of, c_of):
        return (y_of * CORES + c_of) * n_outer + z_of

    def fwd(k):
        return lax.rem(z + k, n_outer)

    def send(src, dst, ssem, rsem, dp_to, v_to):
        return pltpu.make_async_remote_copy(
            src_ref=src,
            dst_ref=dst,
            send_sem=ssem,
            recv_sem=rsem,
            device_id=(dp_to, v_to),
            device_id_type=MESH,
        )

    partner = at(z, y, 1 - c)
    other_y = at(z, 1 - y, c)

    def load(seq):
        return pltpu.make_async_copy(hidden_ref.at[seq], tokens.at[seq], load_sem.at[seq])

    load_positions = pltpu.make_async_copy(positions_hbm, positions_ref, state_sem.at[2])
    load_positions.start()
    load_head = pltpu.make_async_copy(head_hbm, head_ref, state_sem.at[5])
    load_head.start()
    for seq in range(seqs):
        load(seq).start()
    load_labels = pltpu.make_async_copy(labels_hbm, labels_ref, state_sem.at[3])
    load_lse = pltpu.make_async_copy(lse_hbm, lse_ref, state_sem.at[4])
    load_m = pltpu.make_async_copy(m_ref, m_buf, state_sem.at[0])
    load_v = pltpu.make_async_copy(v_ref, v_buf, state_sem.at[1])
    for copy in (load_labels, load_lse, load_m, load_v):
        copy.start()

    sent = []

    def finish():
        for low_k, high_k, copies in sent:

            @pl.loop(low_k, high_k)
            def _(k, copies=copies):
                for copy in copies(k):
                    copy.wait_send()

    barrier = pltpu.get_barrier_semaphore()

    def greet(dp_to, v_to):
        pl.semaphore_signal(barrier, inc=1, device_id=(dp_to, v_to), device_id_type=MESH)

    @pl.loop(1, n_outer)
    def _(k):
        greet(at(fwd(k), y, c), v)

    greet(other_y, v)
    greet(partner, v)
    greet(dp, 1 - v)

    def pick(seq):
        load(seq).wait()
        spots = positions_ref[pl.ds(seq, 1), :]
        hot = lax.broadcasted_iota(jnp.int32, (length, masked), 0) == spots
        picked[seq] = lax.dot_general(
            jnp.where(hot, 1.0, 0.0).astype(BF16),
            tokens[seq],
            (((0,), (0,)), ((), ())),
            preferred_element_type=F32,
        ).astype(BF16)

    def picks(low, high):
        @pl.loop(low, high)
        def _(seq):
            pick(seq)

    load_head.wait()
    pl.semaphore_wait(barrier, n_outer + 2)

    def pair(z_of, y_of, c_of):
        return pieces.at[spot(z_of, y_of, c_of)]

    def piece(z_of, slab):
        return pair(z_of, y, c).at[slab]

    def half_of(h):
        return head_ref[0, :, pl.ds(pl.multiple_of(h * half, half), half)].astype(BF16)

    def x_head():
        return send(across, piece(z, v), all_sent, x_head_recv, dp, 1 - v)

    def outer_copy(z_to, slab):
        ref = piece(z, slab)
        return send(ref, ref, all_sent, outer_recv.at[z], at(z_to, y, c), v)

    def inner_copy(z_of):
        ref = pair(z_of, y, c)
        return send(ref, ref, all_sent, inner_recv.at[z_of], other_y, v)

    def core_copy(z_of, y_of):
        ref = pair(z_of, y_of, c)
        return send(ref, ref, all_sent, core_recv.at[y_of], partner, v)

    def others(d, step):
        for other in (z - d, z + d):

            @pl.when((other >= 0) & (other < n_outer))
            def _(other=other):
                step(other)

    def far_first(step):
        @pl.loop(1, n_outer)
        def _(n):
            others(n_outer - n, step)

    def near_first(step):
        @pl.loop(1, n_outer)
        def _(d):
            others(d, step)

    early, late = 3 * seqs // 5, 4 * seqs // 5
    across[...] = half_of(1 - v)
    pieces[spot(z, y, c), v] = half_of(v)
    x_head().start()
    far_first(lambda z_to: outer_copy(z_to, v).start())
    load_positions.wait()
    picks(0, early)
    whole_head = head_ref[0]
    weight_part = jnp.sum(whole_head * whole_head, axis=(0, 1), keepdims=True)
    send(across, piece(z, 1 - v), all_sent, x_head_recv, dp, 1 - v).wait_recv()
    far_first(lambda z_to: outer_copy(z_to, 1 - v).start())
    inner_copy(z).start()
    core_copy(z, y).start()
    picks(early, late)

    def pass_on(z_from):
        ref = pair(z_from, y, c)
        send(ref, ref, all_sent, outer_recv.at[z_from], dp, 1 - v).wait_recv()
        inner_copy(z_from).start()
        core_copy(z_from, y).start()

    near_first(pass_on)
    picks(late, seqs)
    load_labels.wait()
    load_lse.wait()

    def pass_core(z_from):
        ref = pair(z_from, 1 - y, c)
        send(ref, ref, all_sent, inner_recv.at[z_from], dp, 1 - v).wait_recv()
        core_copy(z_from, 1 - y).start()

    def core_wait(y_of):
        ref = pieces.at[pl.ds(spot(0, y_of, 1 - c), n_outer)]
        send(ref, ref, all_sent, core_recv.at[y_of], dp, 1 - v).wait_recv()

    block = n_dp * 2 * own_rows
    side = block // INNER
    pairs, odd = seqs // 2, seqs % 2
    cut = masked // 2

    def score_part(y_of, seq, count):
        near = pieces[pl.ds(y_of * (n_dp // INNER), n_dp // INNER)].reshape(side, half)
        return lax.dot_general(
            picked[pl.ds(seq, count)].reshape(count * masked, half),
            near,
            (((1,), (1,)), ((), ())),
            preferred_element_type=F32,
        )

    def score_copy(y_of, m):
        return send(
            score_own.at[y_of, m],
            score_other.at[y_of, m],
            all_sent,
            score_recv.at[y_of, m],
            dp,
            1 - v,
        )

    def tail_copy(y_of):
        return send(tail_own.at[y_of], tail_other.at[y_of], all_sent, tail_recv.at[y_of], dp, 1 - v)

    def send_pair(y_of, m):
        both = score_part(y_of, 2 * m, 2)
        score_own[y_of, m] = jnp.concatenate([both[:masked], both[masked:]], axis=1)
        score_copy(y_of, m).start()

    def send_tail(y_of):
        last = score_part(y_of, seqs - 1, 1)
        tail_own[y_of] = jnp.concatenate([last[:cut], last[cut:]], axis=1)
        tail_copy(y_of).start()

    tasks = [functools.partial(send_pair, y, m) for m in range(pairs)]
    if odd:
        tasks.append(functools.partial(send_tail, y))
    pass_core(z)
    core_wait(y)
    for d in range(1, n_outer):
        if tasks:
            tasks.pop(0)()
        others(d, pass_core)
    for task in tasks:
        task()
    core_wait(1 - y)

    @pl.loop(0, pairs)
    def _(m):
        send_pair(1 - y, m)

    if odd:
        send_tail(1 - y)
        sent.append((0, INNER, lambda k: (tail_copy(k),)))
    sent.append((0, pairs, lambda m: (score_copy(0, m), score_copy(1, m))))

    def state_cols(ref):
        return ref.at[0, :, pl.ds(pl.multiple_of((1 - v) * half, half), half)]

    state_copies = [
        send(state_cols(m_ref), state_far.at[0], all_sent, far_recv.at[0], dp, 1 - v),
        send(state_cols(v_ref), state_far.at[1], all_sent, far_recv.at[1], dp, 1 - v),
    ]
    sent.append((0, 1, lambda k: state_copies + [x_head()]))
    sent.append((1, n_outer, lambda k: (outer_copy(z, 0), outer_copy(z, 1))))
    sent.append((0, n_outer, lambda k: (inner_copy(k), core_copy(k, 0), core_copy(k, 1))))

    grads[...] = jnp.zeros_like(grads)
    row = lax.broadcasted_iota(jnp.int32, (block, masked), 0)
    shift = own_rows.bit_length() - 1
    slot = lax.shift_right_logical(row, shift + 1)
    outer_bits = n_outer.bit_length() - 1
    slot_z = slot & (n_outer - 1)
    slot_c = lax.shift_right_logical(slot, outer_bits) & (CORES - 1)
    slot_y = lax.shift_right_logical(slot, outer_bits + CORES.bit_length() - 1)
    row_id = (
        (lax.shift_right_logical(row, shift) & 1) * (n_dp * own_rows)
        + at(slot_z, slot_y, slot_c) * own_rows
        + (row & (own_rows - 1))
    )

    def finish_seq(seq, scores):
        rest = lse_ref[pl.ds(seq, 1), :]
        top = jnp.maximum(jnp.max(scores, axis=0, keepdims=True), rest)
        total = jnp.exp(rest - top) + jnp.sum(jnp.exp(scores - top), axis=0, keepdims=True)
        row_lse = top + jnp.log(total)
        hits = row_id == labels_ref[pl.ds(seq, 1), :]
        target = jnp.sum(jnp.where(hits, scores, 0.0), axis=0, keepdims=True)
        losses_ref[pl.ds(seq, 1), :] = row_lse - target
        logit_grad = (jnp.exp(scores - row_lse) - jnp.where(hits, 1.0, 0.0)).astype(BF16)
        grads[...] += lax.dot_general(
            logit_grad, picked[seq], (((1,), (0,)), ((), ())), preferred_element_type=F32
        ).reshape(n_dp, 2 * own_rows, half)

    @pl.loop(0, pairs)
    def _(m):
        turned = []
        for y_of in range(INNER):
            score_copy(y_of, m).wait_recv()
            turned.append(jnp.transpose(score_own[y_of, m] + score_other[y_of, m]))
        for n in range(2):
            rows = slice(n * side, (n + 1) * side)
            finish_seq(2 * m + n, jnp.concatenate([t[rows] for t in turned], axis=0))

    if odd:
        turned = []
        for y_of in range(INNER):
            tail_copy(y_of).wait_recv()
            turned.append(jnp.transpose(tail_own[y_of] + tail_other[y_of]))
        sides = [jnp.concatenate([t[n * side : (n + 1) * side] for t in turned], axis=0) for n in range(2)]
        finish_seq(seqs - 1, jnp.concatenate(sides, axis=1))

    for copy in state_copies:
        copy.start()

    part = half // 2

    def turn(n):
        down = n_outer - 1 - n
        low_side = jnp.where(down > z, down, down - 1)
        high_side = jnp.where(n < z, n, n + 1)
        return jnp.where(n == n_outer - 1, z, jnp.where(z < n_outer // 2, low_side, high_side))

    def rs_core(d, y_of):
        return send(
            grads.at[spot(d, y_of, 1 - c)],
            got_core.at[d, y_of],
            all_sent,
            rs_core_recv.at[d, y_of],
            partner,
            v,
        )

    def rs_y(d, h):
        return send(send_y.at[d, h], got_y.at[d, h], all_sent, rs_y_recv.at[d, h], other_y, v)

    def rs_z(d, h):
        return send(
            send_z.at[d, h], got_z.at[z, h], all_sent, rs_z_recv.at[z, h], at(d, y, c), v
        )

    def chip_sum(d, y_of, h):
        cols = slice(h * part, (h + 1) * part)
        return grads[spot(d, y_of, c), :, cols] + got_core[d, y_of, :, cols]

    sent.append((0, n_outer, lambda k: (rs_core(k, 0), rs_core(k, 1), rs_y(k, 0), rs_y(k, 1))))
    sent.append((1, n_outer, lambda k: (rs_z(z, 0), rs_z(z, 1))))

    for y_of in (1 - y, y):

        @pl.loop(0, n_outer)
        def _(n, y_of=y_of):
            rs_core(turn(n), y_of).start()

    @pl.loop(0, n_outer)
    def _(n):
        d = turn(n)
        rs_core(d, 1 - y).wait_recv()
        for h in range(2):
            send_y[d, h] = chip_sum(d, 1 - y, h)
            rs_y(d, h).start()

    @pl.loop(0, n_outer - 1)
    def _(n):
        d = turn(n)
        rs_core(d, y).wait_recv()
        for h in range(2):
            rs_y(d, h).wait_recv()
            send_z[d, h] = chip_sum(d, y, h) + got_y[d, h]
            rs_z(d, h).start()

    rs_core(z, y).wait_recv()
    row_halves = []
    for h in range(2):
        rs_y(z, h).wait_recv()
        row_half = chip_sum(z, y, h) + got_y[z, h]
        for k in range(1, n_outer):
            z_from = fwd(k)
            got = got_z.at[z_from, h]
            send(got, got, all_sent, rs_z_recv.at[z_from, h], dp, 1 - v).wait_recv()
            row_half = row_half + got_z[z_from, h]
        row_halves.append(row_half)
    rows8 = jnp.concatenate(row_halves, axis=1)
    low, high = rows8[:own_rows], rows8[own_rows:]
    grad_near = jnp.where(v == 0, low, high)
    grad_far = jnp.where(v == 0, high, low)
    send_x[...] = grad_far
    x_copy = send(send_x, grad_x, all_sent, x_recv, dp, 1 - v)
    x_copy.start()
    sent.append((0, 1, lambda k: (x_copy,)))
    load_m.wait()
    load_v.wait()
    for copy in state_copies:
        copy.wait_recv()

    first_fix = 1.0 - BETA_ONE**STEP
    second_fix = 1.0 - BETA_TWO**STEP

    def lamb(grad, first, second):
        first = BETA_ONE * first + (1.0 - BETA_ONE) * grad
        second = BETA_TWO * second + (1.0 - BETA_TWO) * grad * grad
        update = first / first_fix / (jnp.sqrt(second / second_fix) + ADAM_EPSILON)
        return first, second, update

    def square_sum(values):
        return jnp.sum(values * values, axis=(0, 1), keepdims=True)

    def finish_half(grad, h):
        cols = pl.ds(pl.multiple_of(h * half, half), half)
        first, second, update = lamb(grad, m_buf[0, :, cols], v_buf[0, :, cols])
        new_m_ref[0, :, cols] = first
        new_v_ref[0, :, cols] = second
        update_buf[:, cols] = update
        return update

    lane = lax.broadcasted_iota(jnp.int32, (1, 128), 1)
    _, _, update_far = lamb(grad_far, state_far[0], state_far[1])
    sums_own[1] = jnp.where(lane == 0, square_sum(update_far), 0.0)
    def sum_far(to):
        return send(sums_own.at[1], sums.at[n_dp + dp], all_sent, sum_recv, to, 1 - v)

    def sum_near(to):
        return send(sums_own.at[0], sums.at[dp], all_sent, sum_recv, to, v)

    def near_dp(n):
        return jnp.where(z < n_outer // 2, n_dp - n, n)

    def to_dp(k):
        return lax.rem(dp + k, n_dp)

    @pl.loop(0, n_dp)
    def _(n):
        sum_far(to_dp(near_dp(n))).start()

    near = jnp.where(
        lane == 0,
        square_sum(finish_half(grad_near, v)),
        jnp.where(lane == 1, weight_part, 0.0),
    )
    sums_own[0] = near
    sums[dp] = near

    @pl.loop(1, n_dp)
    def _(n):
        sum_near(to_dp(near_dp(n))).start()

    sent.append((0, n_dp, lambda k: (sum_far(to_dp(k)),)))
    sent.append((1, n_dp, lambda k: (sum_near(to_dp(k)),)))
    x_copy.wait_recv()
    finish_half(grad_x[...], 1 - v)
    finish()
    arrivals = sums.at[pl.ds(0, 2 * n_dp - 1)]
    send(arrivals, arrivals, all_sent, sum_recv, dp, 1 - v).wait_recv()

    totals = jnp.sum(sums[...], axis=0)
    update_total = jnp.sum(jnp.where(lane == 0, totals, 0.0), axis=1, keepdims=True)
    weight_total = jnp.sum(jnp.where(lane == 1, totals, 0.0), axis=1, keepdims=True)
    trust = jnp.sqrt(weight_total) / (jnp.sqrt(update_total) + TRUST_EPSILON)
    new_head_ref[0] = head_ref[0] - LEARNING_RATE * trust * update_buf[...]


def store_kernel(*refs):
    count = (len(refs) - 1) // 2
    sems = refs[-1]
    copies = [
        pltpu.make_async_copy(refs[n], refs[count + n], sems.at[n]) for n in range(count)
    ]
    for copy in copies:
        copy.start()
    for copy in copies:
        copy.wait()


def fused_step(n_dp, hidden, positions, labels, lse_rest, head, m_state, v_state):
    seqs, length, half = hidden.shape
    masked = positions.shape[1]
    own_rows, width = head.shape[1], head.shape[2]
    n_outer = n_dp // (CORES * INNER)
    pair = 2 * own_rows
    block = n_dp * pair
    vmem = pl.BlockSpec(memory_space=pltpu.VMEM)
    anywhere = pl.BlockSpec(memory_space=pltpu.HBM)
    dma = pltpu.SemaphoreType.DMA
    state = jax.ShapeDtypeStruct(head.shape, F32)
    operands = [
        pltpu.with_memory_space_constraint(operand, pltpu.HBM)
        for operand in (hidden, positions, labels, lse_rest, head, m_state, v_state)
    ]
    results = pl.pallas_call(
        functools.partial(step_kernel, n_dp),
        out_shape=(jax.ShapeDtypeStruct(lse_rest.shape, F32), state, state, state),
        in_specs=[anywhere] * 7,
        out_specs=(vmem, vmem, vmem, vmem),
        scratch_shapes=[
            pltpu.VMEM((seqs, length, half), BF16),
            pltpu.VMEM((seqs, masked, half), BF16),
            pltpu.VMEM((n_dp, 2, own_rows, half), BF16),
            pltpu.VMEM((own_rows, half), BF16),
            pltpu.VMEM((INNER, max(seqs // 2, 1), masked, block), F32),
            pltpu.VMEM((INNER, max(seqs // 2, 1), masked, block), F32),
            pltpu.VMEM((INNER, masked // 2, block), F32),
            pltpu.VMEM((INNER, masked // 2, block), F32),
            pltpu.VMEM((n_dp, pair, half), F32),
            pltpu.VMEM((n_outer, INNER, pair, half), F32),
            pltpu.VMEM((n_outer, 2, pair, half // 2), F32),
            pltpu.VMEM((n_outer, 2, pair, half // 2), F32),
            pltpu.VMEM((n_outer, 2, pair, half // 2), F32),
            pltpu.VMEM((n_outer, 2, pair, half // 2), F32),
            pltpu.VMEM((own_rows, half), F32),
            pltpu.VMEM((own_rows, half), F32),
            pltpu.VMEM((2, own_rows, half), F32),
            pltpu.VMEM((1, own_rows, width), F32),
            pltpu.VMEM((1, own_rows, width), F32),
            pltpu.VMEM(positions.shape, jnp.int32),
            pltpu.VMEM(labels.shape, jnp.int32),
            pltpu.VMEM(lse_rest.shape, F32),
            pltpu.VMEM(head.shape, F32),
            pltpu.VMEM((own_rows, width), F32),
            pltpu.VMEM((2, 1, 128), F32),
            pltpu.VMEM((2 * n_dp, 1, 128), F32),
            dma((seqs,)),
            dma((6,)),
            dma,
            dma,
            dma((n_outer,)),
            dma((n_outer,)),
            dma((INNER,)),
            dma((INNER, max(seqs // 2, 1))),
            dma((INNER,)),
            dma((n_outer, INNER)),
            dma((n_outer, 2)),
            dma((n_outer, 2)),
            dma,
            dma,
            dma((2,)),
        ],
        compiler_params=pltpu.CompilerParams(
            collective_id=0, has_side_effects=True, vmem_limit_bytes=48 * 1024 * 1024
        ),
        name="fused_step",
    )(*operands)
    count = len(results)
    return pl.pallas_call(
        store_kernel,
        out_shape=tuple(jax.ShapeDtypeStruct(r.shape, r.dtype) for r in results),
        in_specs=[vmem] * count,
        out_specs=(anywhere,) * count,
        scratch_shapes=[dma((count,))],
        compiler_params=pltpu.CompilerParams(vmem_limit_bytes=4 * 1024 * 1024),
        name="store_results",
    )(*results)


def on_device(hidden, positions, labels, lse_rest, head, m_state, v_state):
    seq_here, mask_here = positions.shape
    rows_here = seq_here * mask_here
    own_rows = head.shape[1]
    model_width = head.shape[2]
    head_own = head.reshape(own_rows, model_width)
    weight_total = lax.psum(jnp.sum(head_own * head_own), "dp")
    local_rows = jnp.take_along_axis(hidden, positions[:, :, None], axis=1).reshape(
        rows_here, hidden.shape[2]
    )
    picked = lax.all_gather(local_rows, "vocab", axis=1, tiled=True)
    head_copy = head_own.astype(jnp.bfloat16)
    scores = lax.dot_general(
        picked,
        lax.all_gather(head_copy, "dp", axis=0, tiled=True),
        (((1,), (1,)), ((), ())),
        preferred_element_type=jnp.float32,
    )
    slab_width = scores.shape[1]
    offset = lax.axis_index("vocab") * slab_width
    label_local = labels.reshape(rows_here) - offset
    label_hits = label_local[:, None] == lax.iota(jnp.int32, slab_width)[None, :]
    target_part = jnp.sum(jnp.where(label_hits, scores, 0.0), axis=1)
    rest_lse = lse_rest.reshape(rows_here)
    slab_max = jnp.max(scores, axis=1)
    block_max = lax.pmax(slab_max, "vocab")
    row_top = jnp.maximum(block_max, rest_lse)
    slab_sum = jnp.sum(jnp.exp(scores - row_top[:, None]), axis=1)
    block_sum, target = lax.psum((slab_sum, target_part), "vocab")
    row_total = block_sum + jnp.exp(rest_lse - row_top)
    row_lse = row_top + jnp.log(row_total)
    losses = (row_lse - target).reshape(seq_here, mask_here)
    logit_grad = (jnp.exp(scores - row_lse[:, None]) - label_hits.astype(jnp.float32)).astype(
        jnp.bfloat16
    )
    full_grad = lax.dot_general(
        logit_grad, picked, (((0,), (0,)), ((), ())), preferred_element_type=jnp.float32
    )
    head_grad = lax.psum_scatter(full_grad, "dp", scatter_dimension=0, tiled=True)
    first_moment = BETA_ONE * m_state.reshape(own_rows, model_width) + (1.0 - BETA_ONE) * head_grad
    second_moment = (
        BETA_TWO * v_state.reshape(own_rows, model_width) + (1.0 - BETA_TWO) * head_grad * head_grad
    )
    first_fix = 1.0 - BETA_ONE**STEP
    second_fix = 1.0 - BETA_TWO**STEP
    update = first_moment / first_fix / (jnp.sqrt(second_moment / second_fix) + ADAM_EPSILON)
    update_part = jnp.sum(update * update)
    update_total = lax.psum(update_part, "dp")
    trust_ratio = jnp.sqrt(weight_total) / (jnp.sqrt(update_total) + TRUST_EPSILON)
    new_head = head_own - LEARNING_RATE * trust_ratio * update
    return (
        losses,
        new_head.reshape(head.shape),
        first_moment.reshape(head.shape),
        second_moment.reshape(head.shape),
    )


def pairwise(mesh, args):
    n_dp, n_vocab = mesh.shape["dp"], mesh.shape["vocab"]
    own_rows = args[4].shape[1] // n_dp
    power_of_two = own_rows & (own_rows - 1) == 0
    n_outer = n_dp // (CORES * INNER)
    power_of_two = power_of_two and n_outer & (n_outer - 1) == 0
    masked = args[1].shape[1]
    power_of_two = power_of_two and masked % 16 == 0
    return n_vocab == 2 and n_dp % (CORES * INNER) == 0 and power_of_two


def solution(mesh):
    def step(*args):
        if pairwise(mesh, args):
            body = functools.partial(fused_step, mesh.shape["dp"])
        else:
            body = on_device
        return sharded(mesh, body)(*args)

    return step


def sharded(mesh, body):
    return jax.shard_map(
        body,
        mesh=mesh,
        in_specs=(
            P("dp", None, "vocab"),
            P("dp", None),
            P("dp", None),
            P("dp", None),
            P("vocab", "dp", None),
            P("vocab", "dp", None),
            P("vocab", "dp", None),
        ),
        out_specs=(
            P("dp", None),
            P("vocab", "dp", None),
            P("vocab", "dp", None),
            P("vocab", "dp", None),
        ),
        check_vma=False,
    )
```

```python
import functools

import jax
import jax.numpy as jnp
from jax import lax
from jax.experimental import pallas as pl
from jax.experimental.pallas import tpu as pltpu
from jax.sharding import PartitionSpec as P

STEP = 100
BETA_ONE = 0.9
BETA_TWO = 0.999
ADAM_EPSILON = 1e-06
TRUST_EPSILON = 1e-06
LEARNING_RATE = 0.02

MESH = pl.DeviceIdType.MESH
CORES = 2
INNER = 2
F32 = jnp.float32
BF16 = jnp.bfloat16


def step_kernel(
    n_dp,
    hidden_ref,
    positions_hbm,
    labels_hbm,
    lse_hbm,
    head_hbm,
    m_ref,
    v_ref,
    losses_ref,
    new_head_ref,
    new_m_ref,
    new_v_ref,
    tokens,
    picked,
    pieces,
    across,
    score_own,
    score_other,
    tail_own,
    tail_other,
    grads,
    got_core,
    last_got_core,
    last_send_z,
    last_got_z,
    last_send_y,
    last_got_y,
    send_y,
    got_y,
    send_z,
    got_z,
    send_x,
    grad_x,
    state_far,
    m_buf,
    v_buf,
    positions_ref,
    labels_ref,
    lse_ref,
    head_ref,
    update_buf,
    sums_own,
    sums,
    load_sem,
    state_sem,
    all_sent,
    x_head_recv,
    outer_recv,
    inner_recv,
    core_recv,
    score_recv,
    tail_recv,
    rs_core_recv,
    last_core_recv,
    last_z_recv,
    last_y_recv,
    rs_y_recv,
    rs_z_recv,
    x_recv,
    sum_recv,
    far_recv,
):
    n_outer = n_dp // (CORES * INNER)
    seqs, length, half = hidden_ref.shape
    masked = positions_ref.shape[1]
    own_rows = head_ref.shape[1]
    dp = lax.axis_index("dp")
    v = lax.axis_index("vocab")
    c = lax.rem(dp, CORES)
    y = lax.rem(lax.div(dp, CORES), INNER)
    z = lax.div(dp, CORES * INNER)

    def at(z_to, y_to, c_to):
        return (z_to * INNER + y_to) * CORES + c_to

    def spot(z_of, y_of, c_of):
        return (y_of * CORES + c_of) * n_outer + z_of

    def fwd(k):
        return lax.rem(z + k, n_outer)

    def send(src, dst, ssem, rsem, dp_to, v_to):
        return pltpu.make_async_remote_copy(
            src_ref=src,
            dst_ref=dst,
            send_sem=ssem,
            recv_sem=rsem,
            device_id=(dp_to, v_to),
            device_id_type=MESH,
        )

    partner = at(z, y, 1 - c)
    other_y = at(z, 1 - y, c)

    def load(seq):
        return pltpu.make_async_copy(hidden_ref.at[seq], tokens.at[seq], load_sem.at[seq])

    load_positions = pltpu.make_async_copy(positions_hbm, positions_ref, state_sem.at[2])
    load_positions.start()
    load_head = pltpu.make_async_copy(head_hbm, head_ref, state_sem.at[5])
    load_head.start()
    for seq in range(seqs):
        load(seq).start()
    load_labels = pltpu.make_async_copy(labels_hbm, labels_ref, state_sem.at[3])
    load_lse = pltpu.make_async_copy(lse_hbm, lse_ref, state_sem.at[4])
    load_m = pltpu.make_async_copy(m_ref, m_buf, state_sem.at[0])
    load_v = pltpu.make_async_copy(v_ref, v_buf, state_sem.at[1])
    for copy in (load_labels, load_lse, load_m, load_v):
        copy.start()

    sent = []

    def finish():
        for low_k, high_k, copies in sent:

            @pl.loop(low_k, high_k)
            def _(k, copies=copies):
                for copy in copies(k):
                    copy.wait_send()

    barrier = pltpu.get_barrier_semaphore()

    def greet(dp_to, v_to):
        pl.semaphore_signal(barrier, inc=1, device_id=(dp_to, v_to), device_id_type=MESH)

    @pl.loop(1, n_outer)
    def _(k):
        greet(at(fwd(k), y, c), v)

    greet(other_y, v)
    greet(partner, v)
    greet(dp, 1 - v)

    def pick(seq):
        load(seq).wait()
        spots = positions_ref[pl.ds(seq, 1), :]
        hot = lax.broadcasted_iota(jnp.int32, (length, masked), 0) == spots
        picked[seq] = lax.dot_general(
            jnp.where(hot, 1.0, 0.0).astype(BF16),
            tokens[seq],
            (((0,), (0,)), ((), ())),
            preferred_element_type=F32,
        ).astype(BF16)

    def picks(low, high):
        @pl.loop(low, high)
        def _(seq):
            pick(seq)

    load_head.wait()
    pl.semaphore_wait(barrier, n_outer + 2)

    def pair(z_of, y_of, c_of):
        return pieces.at[spot(z_of, y_of, c_of)]

    def piece(z_of, slab):
        return pair(z_of, y, c).at[slab]

    def half_of(h):
        return head_ref[0, :, pl.ds(pl.multiple_of(h * half, half), half)].astype(BF16)

    def x_head():
        return send(across, piece(z, v), all_sent, x_head_recv, dp, 1 - v)

    def outer_copy(z_to, slab):
        ref = piece(z, slab)
        return send(ref, ref, all_sent, outer_recv.at[z, slab], at(z_to, y, c), v)

    def inner_copy(z_of, slab):
        ref = piece(z_of, slab)
        return send(ref, ref, all_sent, inner_recv.at[z_of], other_y, v)

    def core_copy(z_of, y_of):
        ref = pair(z_of, y_of, c)
        return send(ref, ref, all_sent, core_recv.at[y_of], partner, v)

    def others(d, step):
        for other in (z - d, z + d):

            @pl.when((other >= 0) & (other < n_outer))
            def _(other=other):
                step(other)

    def far_first(step):
        @pl.loop(1, n_outer)
        def _(n):
            others(n_outer - n, step)

    def near_first(step):
        @pl.loop(1, n_outer)
        def _(d):
            others(d, step)

    early, late = 3 * seqs // 5, 4 * seqs // 5
    across[...] = half_of(1 - v)
    pieces[spot(z, y, c), v] = half_of(v)
    x_head().start()
    far_first(lambda z_to: outer_copy(z_to, v).start())
    inner_copy(z, v).start()
    load_positions.wait()
    picks(0, early)
    whole_head = head_ref[0]
    weight_part = jnp.sum(whole_head * whole_head, axis=(0, 1), keepdims=True)
    send(across, piece(z, 1 - v), all_sent, x_head_recv, dp, 1 - v).wait_recv()
    far_first(lambda z_to: outer_copy(z_to, 1 - v).start())
    inner_copy(z, 1 - v).start()
    core_copy(z, y).start()
    picks(early, late)

    def pass_piece(z_from, slab):
        ref = piece(z_from, slab)
        send(ref, ref, all_sent, outer_recv.at[z_from, slab], dp, 1 - v).wait_recv()
        inner_copy(z_from, slab).start()

    def pass_on(z_from):
        pass_piece(z_from, 1 - v)
        core_copy(z_from, y).start()

    near_first(lambda z_from: pass_piece(z_from, v))
    near_first(pass_on)
    picks(late, seqs)
    load_labels.wait()
    load_lse.wait()

    def pass_core(z_from):
        ref = pair(z_from, 1 - y, c)
        send(ref, ref, all_sent, inner_recv.at[z_from], dp, 1 - v).wait_recv()
        core_copy(z_from, 1 - y).start()

    def core_wait(y_of):
        ref = pieces.at[pl.ds(spot(0, y_of, 1 - c), n_outer)]
        send(ref, ref, all_sent, core_recv.at[y_of], dp, 1 - v).wait_recv()

    block = n_dp * 2 * own_rows
    side = block // INNER
    pairs, odd = seqs // 2, seqs % 2
    cut = masked // 2

    def score_part(y_of, seq, count):
        near = pieces[pl.ds(y_of * (n_dp // INNER), n_dp // INNER)].reshape(side, half)
        return lax.dot_general(
            picked[pl.ds(seq, count)].reshape(count * masked, half),
            near,
            (((1,), (1,)), ((), ())),
            preferred_element_type=F32,
        )

    def score_copy(y_of, m):
        return send(
            score_own.at[y_of, m],
            score_other.at[y_of, m],
            all_sent,
            score_recv.at[y_of, m],
            dp,
            1 - v,
        )

    def tail_copy(y_of):
        return send(tail_own.at[y_of], tail_other.at[y_of], all_sent, tail_recv.at[y_of], dp, 1 - v)

    def send_pair(y_of, m):
        both = score_part(y_of, 2 * m, 2)
        score_own[y_of, m] = jnp.concatenate([both[:masked], both[masked:]], axis=1)
        score_copy(y_of, m).start()

    def send_tail(y_of):
        last = score_part(y_of, seqs - 1, 1)
        tail_own[y_of] = jnp.concatenate([last[:cut], last[cut:]], axis=1)
        tail_copy(y_of).start()

    tasks = [functools.partial(send_pair, y, m) for m in range(pairs)]
    if odd:
        tasks.append(functools.partial(send_tail, y))
    pass_core(z)
    core_wait(y)
    for d in range(1, n_outer):
        if tasks:
            tasks.pop(0)()
        others(d, pass_core)
    for task in tasks:
        task()
    core_wait(1 - y)

    @pl.loop(0, pairs)
    def _(m):
        send_pair(1 - y, m)

    if odd:
        send_tail(1 - y)
        sent.append((0, INNER, lambda k: (tail_copy(k),)))
    sent.append((0, pairs, lambda m: (score_copy(0, m), score_copy(1, m))))

    def state_cols(ref):
        return ref.at[0, :, pl.ds(pl.multiple_of((1 - v) * half, half), half)]

    state_copies = [
        send(state_cols(m_ref), state_far.at[0], all_sent, far_recv.at[0], dp, 1 - v),
        send(state_cols(v_ref), state_far.at[1], all_sent, far_recv.at[1], dp, 1 - v),
    ]
    sent.append((0, 1, lambda k: state_copies + [x_head()]))
    sent.append((1, n_outer, lambda k: (outer_copy(z, 0), outer_copy(z, 1))))
    sent.append((0, n_outer, lambda k: (inner_copy(k, 0), inner_copy(k, 1), core_copy(k, 0), core_copy(k, 1))))

    grads[...] = jnp.zeros_like(grads)
    row = lax.broadcasted_iota(jnp.int32, (block, masked), 0)
    shift = own_rows.bit_length() - 1
    slot = lax.shift_right_logical(row, shift + 1)
    outer_bits = n_outer.bit_length() - 1
    slot_z = slot & (n_outer - 1)
    slot_c = lax.shift_right_logical(slot, outer_bits) & (CORES - 1)
    slot_y = lax.shift_right_logical(slot, outer_bits + CORES.bit_length() - 1)
    row_id = (
        (lax.shift_right_logical(row, shift) & 1) * (n_dp * own_rows)
        + at(slot_z, slot_y, slot_c) * own_rows
        + (row & (own_rows - 1))
    )

    def finish_seq(seq, scores):
        rest = lse_ref[pl.ds(seq, 1), :]
        top = jnp.maximum(jnp.max(scores, axis=0, keepdims=True), rest)
        total = jnp.exp(rest - top) + jnp.sum(jnp.exp(scores - top), axis=0, keepdims=True)
        row_lse = top + jnp.log(total)
        hits = row_id == labels_ref[pl.ds(seq, 1), :]
        target = jnp.sum(jnp.where(hits, scores, 0.0), axis=0, keepdims=True)
        losses_ref[pl.ds(seq, 1), :] = row_lse - target
        logit_grad = (jnp.exp(scores - row_lse) - jnp.where(hits, 1.0, 0.0)).astype(BF16)
        grads[...] += lax.dot_general(
            logit_grad, picked[seq], (((1,), (0,)), ((), ())), preferred_element_type=F32
        ).reshape(n_dp, 2 * own_rows, half)

    @pl.loop(0, pairs)
    def _(m):
        turned = []
        for y_of in range(INNER):
            score_copy(y_of, m).wait_recv()
            turned.append(jnp.transpose(score_own[y_of, m] + score_other[y_of, m]))
        for n in range(2):
            rows = slice(n * side, (n + 1) * side)
            finish_seq(2 * m + n, jnp.concatenate([t[rows] for t in turned], axis=0))

    if odd:
        turned = []
        for y_of in range(INNER):
            tail_copy(y_of).wait_recv()
            turned.append(jnp.transpose(tail_own[y_of] + tail_other[y_of]))
        sides = [jnp.concatenate([t[n * side : (n + 1) * side] for t in turned], axis=0) for n in range(2)]
        finish_seq(seqs - 1, jnp.concatenate(sides, axis=1))

    for copy in state_copies:
        copy.start()

    quarter = half // 4
    main = half - quarter
    part = main // 2

    def turn(n):
        down = n_outer - 1 - n
        low_side = jnp.where(down > z, down, down - 1)
        high_side = jnp.where(n < z, n, n + 1)
        return jnp.where(n == n_outer - 1, z, jnp.where(z < n_outer // 2, low_side, high_side))

    def rs_core(d, y_of):
        return send(
            grads.at[spot(d, y_of, 1 - c), :, pl.ds(0, main)],
            got_core.at[d, y_of],
            all_sent,
            rs_core_recv.at[d, y_of],
            partner,
            v,
        )

    def rs_y(d, h):
        return send(send_y.at[d, h], got_y.at[d, h], all_sent, rs_y_recv.at[d, h], other_y, v)

    def rs_z(d, h):
        return send(
            send_z.at[d, h], got_z.at[z, h], all_sent, rs_z_recv.at[z, h], at(d, y, c), v
        )

    def chip_sum(d, y_of, h):
        cols = slice(h * part, (h + 1) * part)
        return grads[spot(d, y_of, c), :, cols] + got_core[d, y_of, :, cols]

    def last_core(y_of):
        return send(
            grads.at[pl.ds(spot(0, y_of, 1 - c), n_outer), :, pl.ds(main, quarter)],
            last_got_core.at[y_of],
            all_sent,
            last_core_recv.at[y_of],
            partner,
            v,
        )

    def last_z(d):
        return send(
            last_send_z.at[d], last_got_z.at[z], all_sent, last_z_recv.at[z], at(d, y, c), v
        )

    def last_sum(d, y_of):
        return grads[spot(d, y_of, c), :, pl.ds(main, quarter)] + last_got_core[y_of, d]

    last_y = send(last_send_y, last_got_y, all_sent, last_y_recv, other_y, v)
    sent.append((0, n_outer, lambda k: (rs_core(k, 0), rs_core(k, 1), rs_y(k, 0), rs_y(k, 1))))
    sent.append((1, n_outer, lambda k: (rs_z(z, 0), rs_z(z, 1), last_z(z))))
    sent.append((0, 1, lambda k: (last_core(0), last_core(1), last_y)))

    rs_core(turn(0), 1 - y).start()
    for y_of in range(INNER):
        last_core(y_of).start()

    @pl.loop(1, n_outer)
    def _(n):
        rs_core(turn(n), 1 - y).start()

    @pl.loop(0, n_outer)
    def _(n):
        rs_core(turn(n), y).start()

    def send_other(n):
        d = turn(n)
        rs_core(d, 1 - y).wait_recv()
        for h in range(2):
            send_y[d, h] = chip_sum(d, 1 - y, h)
            rs_y(d, h).start()

    send_other(0)
    for y_of in range(INNER):
        last_core(y_of).wait_recv()

    @pl.loop(0, n_outer - 1)
    def _(n):
        d = turn(n)
        for y_of in range(INNER):
            last_send_z[d, y_of] = last_sum(d, y_of)
        last_z(d).start()

    @pl.loop(1, n_outer)
    def _(n):
        send_other(n)

    @pl.loop(0, n_outer - 1)
    def _(n):
        d = turn(n)
        rs_core(d, y).wait_recv()
        for h in range(2):
            rs_y(d, h).wait_recv()
            send_z[d, h] = chip_sum(d, y, h) + got_y[d, h]
            rs_z(d, h).start()

    last_own, last_other = last_sum(z, y), last_sum(z, 1 - y)
    for k in range(1, n_outer):
        z_from = fwd(k)
        got = last_got_z.at[z_from]
        send(got, got, all_sent, last_z_recv.at[z_from], dp, 1 - v).wait_recv()
        last_own = last_own + last_got_z[z_from, y]
        last_other = last_other + last_got_z[z_from, 1 - y]
    last_send_y[...] = last_other
    last_y.start()
    rs_core(z, y).wait_recv()
    row_halves = []
    for h in range(2):
        rs_y(z, h).wait_recv()
        row_half = chip_sum(z, y, h) + got_y[z, h]
        for k in range(1, n_outer):
            z_from = fwd(k)
            got = got_z.at[z_from, h]
            send(got, got, all_sent, rs_z_recv.at[z_from, h], dp, 1 - v).wait_recv()
            row_half = row_half + got_z[z_from, h]
        row_halves.append(row_half)
    last_y.wait_recv()
    rows8 = jnp.concatenate([*row_halves, last_own + last_got_y[...]], axis=1)
    low, high = rows8[:own_rows], rows8[own_rows:]
    grad_near = jnp.where(v == 0, low, high)
    grad_far = jnp.where(v == 0, high, low)
    send_x[...] = grad_far
    x_copy = send(send_x, grad_x, all_sent, x_recv, dp, 1 - v)
    x_copy.start()
    sent.append((0, 1, lambda k: (x_copy,)))
    load_m.wait()
    load_v.wait()
    for copy in state_copies:
        copy.wait_recv()

    first_fix = 1.0 - BETA_ONE**STEP
    second_fix = 1.0 - BETA_TWO**STEP

    def lamb(grad, first, second):
        first = BETA_ONE * first + (1.0 - BETA_ONE) * grad
        second = BETA_TWO * second + (1.0 - BETA_TWO) * grad * grad
        update = first / first_fix / (jnp.sqrt(second / second_fix) + ADAM_EPSILON)
        return first, second, update

    def square_sum(values):
        return jnp.sum(values * values, axis=(0, 1), keepdims=True)

    def finish_half(grad, h):
        cols = pl.ds(pl.multiple_of(h * half, half), half)
        first, second, update = lamb(grad, m_buf[0, :, cols], v_buf[0, :, cols])
        new_m_ref[0, :, cols] = first
        new_v_ref[0, :, cols] = second
        update_buf[:, cols] = update
        return update

    lane = lax.broadcasted_iota(jnp.int32, (1, 128), 1)
    _, _, update_far = lamb(grad_far, state_far[0], state_far[1])
    sums_own[1] = jnp.where(lane == 0, square_sum(update_far), 0.0)
    def sum_far(to):
        return send(sums_own.at[1], sums.at[n_dp + dp], all_sent, sum_recv, to, 1 - v)

    def sum_near(to):
        return send(sums_own.at[0], sums.at[dp], all_sent, sum_recv, to, v)

    def near_dp(n):
        return jnp.where(z < n_outer // 2, n_dp - n, n)

    def to_dp(k):
        return lax.rem(dp + k, n_dp)

    @pl.loop(0, n_dp)
    def _(n):
        sum_far(to_dp(near_dp(n))).start()

    near = jnp.where(
        lane == 0,
        square_sum(finish_half(grad_near, v)),
        jnp.where(lane == 1, weight_part, 0.0),
    )
    sums_own[0] = near
    sums[dp] = near

    @pl.loop(1, n_dp)
    def _(n):
        sum_near(to_dp(near_dp(n))).start()

    sent.append((0, n_dp, lambda k: (sum_far(to_dp(k)),)))
    sent.append((1, n_dp, lambda k: (sum_near(to_dp(k)),)))
    x_copy.wait_recv()
    finish_half(grad_x[...], 1 - v)
    finish()
    arrivals = sums.at[pl.ds(0, 2 * n_dp - 1)]
    send(arrivals, arrivals, all_sent, sum_recv, dp, 1 - v).wait_recv()

    totals = jnp.sum(sums[...], axis=0)
    update_total = jnp.sum(jnp.where(lane == 0, totals, 0.0), axis=1, keepdims=True)
    weight_total = jnp.sum(jnp.where(lane == 1, totals, 0.0), axis=1, keepdims=True)
    trust = jnp.sqrt(weight_total) / (jnp.sqrt(update_total) + TRUST_EPSILON)
    new_head_ref[0] = head_ref[0] - LEARNING_RATE * trust * update_buf[...]


def store_kernel(*refs):
    count = (len(refs) - 1) // 2
    sems = refs[-1]
    copies = [
        pltpu.make_async_copy(refs[n], refs[count + n], sems.at[n]) for n in range(count)
    ]
    for copy in copies:
        copy.start()
    for copy in copies:
        copy.wait()


def fused_step(n_dp, hidden, positions, labels, lse_rest, head, m_state, v_state):
    seqs, length, half = hidden.shape
    masked = positions.shape[1]
    own_rows, width = head.shape[1], head.shape[2]
    n_outer = n_dp // (CORES * INNER)
    pair = 2 * own_rows
    quarter = half // 4
    block = n_dp * pair
    vmem = pl.BlockSpec(memory_space=pltpu.VMEM)
    anywhere = pl.BlockSpec(memory_space=pltpu.HBM)
    dma = pltpu.SemaphoreType.DMA
    state = jax.ShapeDtypeStruct(head.shape, F32)
    operands = [
        pltpu.with_memory_space_constraint(operand, pltpu.HBM)
        for operand in (hidden, positions, labels, lse_rest, head, m_state, v_state)
    ]
    results = pl.pallas_call(
        functools.partial(step_kernel, n_dp),
        out_shape=(jax.ShapeDtypeStruct(lse_rest.shape, F32), state, state, state),
        in_specs=[anywhere] * 7,
        out_specs=(vmem, vmem, vmem, vmem),
        scratch_shapes=[
            pltpu.VMEM((seqs, length, half), BF16),
            pltpu.VMEM((seqs, masked, half), BF16),
            pltpu.VMEM((n_dp, 2, own_rows, half), BF16),
            pltpu.VMEM((own_rows, half), BF16),
            pltpu.VMEM((INNER, max(seqs // 2, 1), masked, block), F32),
            pltpu.VMEM((INNER, max(seqs // 2, 1), masked, block), F32),
            pltpu.VMEM((INNER, masked // 2, block), F32),
            pltpu.VMEM((INNER, masked // 2, block), F32),
            pltpu.VMEM((n_dp, pair, half), F32),
            pltpu.VMEM((n_outer, INNER, pair, half - quarter), F32),
            pltpu.VMEM((INNER, n_outer, pair, quarter), F32),
            pltpu.VMEM((n_outer, INNER, pair, quarter), F32),
            pltpu.VMEM((n_outer, INNER, pair, quarter), F32),
            pltpu.VMEM((pair, quarter), F32),
            pltpu.VMEM((pair, quarter), F32),
            pltpu.VMEM((n_outer, 2, pair, (half - quarter) // 2), F32),
            pltpu.VMEM((n_outer, 2, pair, (half - quarter) // 2), F32),
            pltpu.VMEM((n_outer, 2, pair, (half - quarter) // 2), F32),
            pltpu.VMEM((n_outer, 2, pair, (half - quarter) // 2), F32),
            pltpu.VMEM((own_rows, half), F32),
            pltpu.VMEM((own_rows, half), F32),
            pltpu.VMEM((2, own_rows, half), F32),
            pltpu.VMEM((1, own_rows, width), F32),
            pltpu.VMEM((1, own_rows, width), F32),
            pltpu.VMEM(positions.shape, jnp.int32),
            pltpu.VMEM(labels.shape, jnp.int32),
            pltpu.VMEM(lse_rest.shape, F32),
            pltpu.VMEM(head.shape, F32),
            pltpu.VMEM((own_rows, width), F32),
            pltpu.VMEM((2, 1, 128), F32),
            pltpu.VMEM((2 * n_dp, 1, 128), F32),
            dma((seqs,)),
            dma((6,)),
            dma,
            dma,
            dma((n_outer, 2)),
            dma((n_outer,)),
            dma((INNER,)),
            dma((INNER, max(seqs // 2, 1))),
            dma((INNER,)),
            dma((n_outer, INNER)),
            dma((INNER,)),
            dma((n_outer,)),
            dma,
            dma((n_outer, 2)),
            dma((n_outer, 2)),
            dma,
            dma,
            dma((2,)),
        ],
        compiler_params=pltpu.CompilerParams(
            collective_id=0, has_side_effects=True, vmem_limit_bytes=48 * 1024 * 1024
        ),
        name="fused_step",
    )(*operands)
    count = len(results)
    return pl.pallas_call(
        store_kernel,
        out_shape=tuple(jax.ShapeDtypeStruct(r.shape, r.dtype) for r in results),
        in_specs=[vmem] * count,
        out_specs=(anywhere,) * count,
        scratch_shapes=[dma((count,))],
        compiler_params=pltpu.CompilerParams(vmem_limit_bytes=4 * 1024 * 1024),
        name="store_results",
    )(*results)


def on_device(hidden, positions, labels, lse_rest, head, m_state, v_state):
    seq_here, mask_here = positions.shape
    rows_here = seq_here * mask_here
    own_rows = head.shape[1]
    model_width = head.shape[2]
    head_own = head.reshape(own_rows, model_width)
    weight_total = lax.psum(jnp.sum(head_own * head_own), "dp")
    local_rows = jnp.take_along_axis(hidden, positions[:, :, None], axis=1).reshape(
        rows_here, hidden.shape[2]
    )
    picked = lax.all_gather(local_rows, "vocab", axis=1, tiled=True)
    head_copy = head_own.astype(jnp.bfloat16)
    scores = lax.dot_general(
        picked,
        lax.all_gather(head_copy, "dp", axis=0, tiled=True),
        (((1,), (1,)), ((), ())),
        preferred_element_type=jnp.float32,
    )
    slab_width = scores.shape[1]
    offset = lax.axis_index("vocab") * slab_width
    label_local = labels.reshape(rows_here) - offset
    label_hits = label_local[:, None] == lax.iota(jnp.int32, slab_width)[None, :]
    target_part = jnp.sum(jnp.where(label_hits, scores, 0.0), axis=1)
    rest_lse = lse_rest.reshape(rows_here)
    slab_max = jnp.max(scores, axis=1)
    block_max = lax.pmax(slab_max, "vocab")
    row_top = jnp.maximum(block_max, rest_lse)
    slab_sum = jnp.sum(jnp.exp(scores - row_top[:, None]), axis=1)
    block_sum, target = lax.psum((slab_sum, target_part), "vocab")
    row_total = block_sum + jnp.exp(rest_lse - row_top)
    row_lse = row_top + jnp.log(row_total)
    losses = (row_lse - target).reshape(seq_here, mask_here)
    logit_grad = (jnp.exp(scores - row_lse[:, None]) - label_hits.astype(jnp.float32)).astype(
        jnp.bfloat16
    )
    full_grad = lax.dot_general(
        logit_grad, picked, (((0,), (0,)), ((), ())), preferred_element_type=jnp.float32
    )
    head_grad = lax.psum_scatter(full_grad, "dp", scatter_dimension=0, tiled=True)
    first_moment = BETA_ONE * m_state.reshape(own_rows, model_width) + (1.0 - BETA_ONE) * head_grad
    second_moment = (
        BETA_TWO * v_state.reshape(own_rows, model_width) + (1.0 - BETA_TWO) * head_grad * head_grad
    )
    first_fix = 1.0 - BETA_ONE**STEP
    second_fix = 1.0 - BETA_TWO**STEP
    update = first_moment / first_fix / (jnp.sqrt(second_moment / second_fix) + ADAM_EPSILON)
    update_part = jnp.sum(update * update)
    update_total = lax.psum(update_part, "dp")
    trust_ratio = jnp.sqrt(weight_total) / (jnp.sqrt(update_total) + TRUST_EPSILON)
    new_head = head_own - LEARNING_RATE * trust_ratio * update
    return (
        losses,
        new_head.reshape(head.shape),
        first_moment.reshape(head.shape),
        second_moment.reshape(head.shape),
    )


def pairwise(mesh, args):
    n_dp, n_vocab = mesh.shape["dp"], mesh.shape["vocab"]
    own_rows = args[4].shape[1] // n_dp
    power_of_two = own_rows & (own_rows - 1) == 0
    n_outer = n_dp // (CORES * INNER)
    power_of_two = power_of_two and n_outer & (n_outer - 1) == 0
    masked, width = args[1].shape[1], args[4].shape[2]
    power_of_two = power_of_two and masked % 16 == 0 and width % 2048 == 0
    return n_vocab == 2 and n_dp % (CORES * INNER) == 0 and power_of_two


def solution(mesh):
    def step(*args):
        if pairwise(mesh, args):
            body = functools.partial(fused_step, mesh.shape["dp"])
        else:
            body = on_device
        return sharded(mesh, body)(*args)

    return step


def sharded(mesh, body):
    return jax.shard_map(
        body,
        mesh=mesh,
        in_specs=(
            P("dp", None, "vocab"),
            P("dp", None),
            P("dp", None),
            P("dp", None),
            P("vocab", "dp", None),
            P("vocab", "dp", None),
            P("vocab", "dp", None),
        ),
        out_specs=(
            P("dp", None),
            P("vocab", "dp", None),
            P("vocab", "dp", None),
            P("vocab", "dp", None),
        ),
        check_vma=False,
    )
```

```python
import functools

import jax
import jax.numpy as jnp
from jax import lax
from jax.experimental import pallas as pl
from jax.experimental.pallas import tpu as pltpu
from jax.sharding import PartitionSpec as P

STEP = 100
BETA_ONE = 0.9
BETA_TWO = 0.999
ADAM_EPSILON = 1e-06
TRUST_EPSILON = 1e-06
LEARNING_RATE = 0.02

MESH = pl.DeviceIdType.MESH
CORES = 2
INNER = 2
PARTS = 1
F32 = jnp.float32
BF16 = jnp.bfloat16


def step_kernel(
    n_dp,
    hidden_ref,
    positions_hbm,
    labels_hbm,
    lse_hbm,
    head_hbm,
    m_ref,
    v_ref,
    losses_ref,
    new_head_ref,
    new_m_ref,
    new_v_ref,
    tokens,
    picked,
    pieces,
    across,
    score_own,
    score_other,
    tail_own,
    tail_other,
    grads,
    got_core,
    last_got_core,
    last_send_z,
    last_got_z,
    last_send_y,
    last_got_y,
    send_y,
    got_y,
    send_z,
    got_z,
    send_x,
    grad_x,
    state_far,
    m_buf,
    v_buf,
    positions_ref,
    labels_ref,
    lse_ref,
    head_ref,
    update_buf,
    sums_own,
    sums,
    load_sem,
    state_sem,
    all_sent,
    x_head_recv,
    outer_recv,
    inner_recv,
    core_recv,
    score_recv,
    tail_recv,
    rs_core_recv,
    last_core_recv,
    last_z_recv,
    last_y_recv,
    rs_y_recv,
    rs_z_recv,
    x_recv,
    sum_recv,
    far_recv,
):
    n_outer = n_dp // (CORES * INNER)
    seqs, length, half = hidden_ref.shape
    masked = positions_ref.shape[1]
    own_rows = head_ref.shape[1]
    dp = lax.axis_index("dp")
    v = lax.axis_index("vocab")
    c = lax.rem(dp, CORES)
    y = lax.rem(lax.div(dp, CORES), INNER)
    z = lax.div(dp, CORES * INNER)

    def at(z_to, y_to, c_to):
        return (z_to * INNER + y_to) * CORES + c_to

    def spot(z_of, y_of, c_of):
        return (y_of * CORES + c_of) * n_outer + z_of

    def fwd(k):
        return lax.rem(z + k, n_outer)

    def send(src, dst, ssem, rsem, dp_to, v_to):
        return pltpu.make_async_remote_copy(
            src_ref=src,
            dst_ref=dst,
            send_sem=ssem,
            recv_sem=rsem,
            device_id=(dp_to, v_to),
            device_id_type=MESH,
        )

    partner = at(z, y, 1 - c)
    other_y = at(z, 1 - y, c)

    def load(seq):
        return pltpu.make_async_copy(hidden_ref.at[seq], tokens.at[seq], load_sem.at[seq])

    load_positions = pltpu.make_async_copy(positions_hbm, positions_ref, state_sem.at[2])
    load_positions.start()
    load_head = pltpu.make_async_copy(head_hbm, head_ref, state_sem.at[5])
    load_head.start()
    for seq in range(seqs):
        load(seq).start()
    load_labels = pltpu.make_async_copy(labels_hbm, labels_ref, state_sem.at[3])
    load_lse = pltpu.make_async_copy(lse_hbm, lse_ref, state_sem.at[4])
    load_m = pltpu.make_async_copy(m_ref, m_buf, state_sem.at[0])
    load_v = pltpu.make_async_copy(v_ref, v_buf, state_sem.at[1])
    for copy in (load_labels, load_lse, load_m, load_v):
        copy.start()

    sent = []

    def finish():
        for low_k, high_k, copies in sent:

            @pl.loop(low_k, high_k)
            def _(k, copies=copies):
                for copy in copies(k):
                    copy.wait_send()

    barrier = pltpu.get_barrier_semaphore()

    def greet(dp_to, v_to):
        pl.semaphore_signal(barrier, inc=1, device_id=(dp_to, v_to), device_id_type=MESH)

    @pl.loop(1, n_outer)
    def _(k):
        greet(at(fwd(k), y, c), v)

    greet(other_y, v)
    greet(partner, v)
    greet(dp, 1 - v)

    def pick(seq):
        load(seq).wait()
        spots = positions_ref[pl.ds(seq, 1), :]
        hot = lax.broadcasted_iota(jnp.int32, (length, masked), 0) == spots
        picked[seq] = lax.dot_general(
            jnp.where(hot, 1.0, 0.0).astype(BF16),
            tokens[seq],
            (((0,), (0,)), ((), ())),
            preferred_element_type=F32,
        ).astype(BF16)

    def picks(low, high):
        @pl.loop(low, high)
        def _(seq):
            pick(seq)

    load_head.wait()
    pl.semaphore_wait(barrier, n_outer + 2)

    def pair(z_of, y_of, c_of):
        return pieces.at[spot(z_of, y_of, c_of)]

    def piece(z_of, slab):
        return pair(z_of, y, c).at[slab]

    def half_of(h):
        return head_ref[0, :, pl.ds(pl.multiple_of(h * half, half), half)].astype(BF16)

    def x_head():
        return send(across, piece(z, v), all_sent, x_head_recv, dp, 1 - v)

    def outer_copy(z_to, slab):
        ref = piece(z, slab)
        return send(ref, ref, all_sent, outer_recv.at[z, slab], at(z_to, y, c), v)

    def inner_copy(z_of, slab):
        ref = piece(z_of, slab)
        return send(ref, ref, all_sent, inner_recv.at[z_of], other_y, v)

    def core_copy(z_of, y_of):
        ref = pair(z_of, y_of, c)
        return send(ref, ref, all_sent, core_recv.at[y_of], partner, v)

    def others(d, step):
        for other in (z - d, z + d):

            @pl.when((other >= 0) & (other < n_outer))
            def _(other=other):
                step(other)

    def far_first(step):
        @pl.loop(1, n_outer)
        def _(n):
            others(n_outer - n, step)

    def near_first(step):
        @pl.loop(1, n_outer)
        def _(d):
            others(d, step)

    early, late = 3 * seqs // 5, 4 * seqs // 5
    across[...] = half_of(1 - v)
    pieces[spot(z, y, c), v] = half_of(v)
    x_head().start()
    far_first(lambda z_to: outer_copy(z_to, v).start())
    inner_copy(z, v).start()
    load_positions.wait()
    picks(0, early)
    whole_head = head_ref[0]
    weight_part = jnp.sum(whole_head * whole_head, axis=(0, 1), keepdims=True)
    send(across, piece(z, 1 - v), all_sent, x_head_recv, dp, 1 - v).wait_recv()
    far_first(lambda z_to: outer_copy(z_to, 1 - v).start())
    inner_copy(z, 1 - v).start()
    core_copy(z, y).start()
    picks(early, late)

    def pass_piece(z_from, slab):
        ref = piece(z_from, slab)
        send(ref, ref, all_sent, outer_recv.at[z_from, slab], dp, 1 - v).wait_recv()
        inner_copy(z_from, slab).start()

    def pass_on(z_from):
        pass_piece(z_from, 1 - v)
        core_copy(z_from, y).start()

    near_first(lambda z_from: pass_piece(z_from, v))
    picks(late, seqs)
    near_first(pass_on)
    load_labels.wait()
    load_lse.wait()

    def pass_core(z_from):
        ref = pair(z_from, 1 - y, c)
        send(ref, ref, all_sent, inner_recv.at[z_from], dp, 1 - v).wait_recv()
        core_copy(z_from, 1 - y).start()

    def core_wait(y_of):
        ref = pieces.at[pl.ds(spot(0, y_of, 1 - c), n_outer)]
        send(ref, ref, all_sent, core_recv.at[y_of], dp, 1 - v).wait_recv()

    block = n_dp * 2 * own_rows
    side = block // INNER
    pairs, odd = seqs // 2, seqs % 2
    cut = masked // 2

    def score_part(y_of, seq, count):
        near = pieces[pl.ds(y_of * (n_dp // INNER), n_dp // INNER)].reshape(side, half)
        return lax.dot_general(
            picked[pl.ds(seq, count)].reshape(count * masked, half),
            near,
            (((1,), (1,)), ((), ())),
            preferred_element_type=F32,
        )

    def score_copy(y_of, m):
        return send(
            score_own.at[y_of, m],
            score_other.at[y_of, m],
            all_sent,
            score_recv.at[y_of, m],
            dp,
            1 - v,
        )

    def tail_copy(y_of):
        return send(tail_own.at[y_of], tail_other.at[y_of], all_sent, tail_recv.at[y_of], dp, 1 - v)

    def send_pair(y_of, m):
        both = score_part(y_of, 2 * m, 2)
        score_own[y_of, m] = jnp.concatenate([both[:masked], both[masked:]], axis=1)
        score_copy(y_of, m).start()

    def send_tail(y_of):
        last = score_part(y_of, seqs - 1, 1)
        tail_own[y_of] = jnp.concatenate([last[:cut], last[cut:]], axis=1)
        tail_copy(y_of).start()

    tasks = [functools.partial(send_pair, y, m) for m in range(pairs)]
    if odd:
        tasks.append(functools.partial(send_tail, y))
    pass_core(z)
    core_wait(y)
    for d in range(1, n_outer):
        if tasks:
            tasks.pop(0)()
        others(d, pass_core)
    for task in tasks:
        task()
    core_wait(1 - y)

    @pl.loop(0, pairs)
    def _(m):
        send_pair(1 - y, m)

    if odd:
        send_tail(1 - y)
        sent.append((0, INNER, lambda k: (tail_copy(k),)))
    sent.append((0, pairs, lambda m: (score_copy(0, m), score_copy(1, m))))

    def state_cols(ref):
        return ref.at[0, :, pl.ds(pl.multiple_of((1 - v) * half, half), half)]

    state_copies = [
        send(state_cols(m_ref), state_far.at[0], all_sent, far_recv.at[0], dp, 1 - v),
        send(state_cols(v_ref), state_far.at[1], all_sent, far_recv.at[1], dp, 1 - v),
    ]
    sent.append((0, 1, lambda k: state_copies + [x_head()]))
    sent.append((1, n_outer, lambda k: (outer_copy(z, 0), outer_copy(z, 1))))
    sent.append((0, n_outer, lambda k: (inner_copy(k, 0), inner_copy(k, 1), core_copy(k, 0), core_copy(k, 1))))

    row = lax.broadcasted_iota(jnp.int32, (block, masked), 0)
    shift = own_rows.bit_length() - 1
    slot = lax.shift_right_logical(row, shift + 1)
    outer_bits = n_outer.bit_length() - 1
    slot_z = slot & (n_outer - 1)
    slot_c = lax.shift_right_logical(slot, outer_bits) & (CORES - 1)
    slot_y = lax.shift_right_logical(slot, outer_bits + CORES.bit_length() - 1)
    row_id = (
        (lax.shift_right_logical(row, shift) & 1) * (n_dp * own_rows)
        + at(slot_z, slot_y, slot_c) * own_rows
        + (row & (own_rows - 1))
    )

    def logit_grad(seq, scores):
        rest = lse_ref[pl.ds(seq, 1), :]
        top = jnp.maximum(jnp.max(scores, axis=0, keepdims=True), rest)
        exps = jnp.exp(scores - top)
        total = jnp.exp(rest - top) + jnp.sum(exps, axis=0, keepdims=True)
        hits = row_id == labels_ref[pl.ds(seq, 1), :]
        target = jnp.sum(jnp.where(hits, scores, 0.0), axis=0, keepdims=True)
        losses_ref[pl.ds(seq, 1), :] = top + jnp.log(total) - target
        return exps * (1.0 / total) - jnp.where(hits, 1.0, 0.0)

    def add_grads(seq, count, logits):
        new = lax.dot_general(
            logits.astype(BF16),
            picked[pl.ds(seq, count)].reshape(count * masked, half),
            (((1,), (0,)), ((), ())),
            preferred_element_type=F32,
        ).reshape(n_dp, 2 * own_rows, half)
        grads[...] = new if seq == 0 else grads[...] + new

    for m in range(pairs):
        turned = []
        for y_of in range(INNER):
            score_copy(y_of, m).wait_recv()
            turned.append(jnp.transpose(score_own[y_of, m] + score_other[y_of, m]))
        logits = []
        for n in range(2):
            rows = slice(n * side, (n + 1) * side)
            logits.append(logit_grad(2 * m + n, jnp.concatenate([t[rows] for t in turned], axis=0)))
        add_grads(2 * m, 2, jnp.concatenate(logits, axis=1))

    if odd:
        turned = []
        for y_of in range(INNER):
            tail_copy(y_of).wait_recv()
            turned.append(jnp.transpose(tail_own[y_of] + tail_other[y_of]))
        sides = [jnp.concatenate([t[n * side : (n + 1) * side] for t in turned], axis=0) for n in range(2)]
        add_grads(seqs - 1, 1, logit_grad(seqs - 1, jnp.concatenate(sides, axis=1)))

    for copy in state_copies:
        copy.start()

    quarter = half // 4
    main = half - quarter
    part = main // PARTS

    def turn(n):
        down = n_outer - 1 - n
        low_side = jnp.where(down > z, down, down - 1)
        high_side = jnp.where(n < z, n, n + 1)
        return jnp.where(n == n_outer - 1, z, jnp.where(z < n_outer // 2, low_side, high_side))

    def rs_core(d, y_of):
        return send(
            grads.at[spot(d, y_of, 1 - c), :, pl.ds(0, main)],
            got_core.at[d, y_of],
            all_sent,
            rs_core_recv.at[d, y_of],
            partner,
            v,
        )

    def rs_y(d, h):
        return send(send_y.at[d, h], got_y.at[d, h], all_sent, rs_y_recv.at[d, h], other_y, v)

    def rs_z(d, h):
        return send(
            send_z.at[d, h], got_z.at[z, h], all_sent, rs_z_recv.at[z, h], at(d, y, c), v
        )

    def chip_sum(d, y_of, h):
        cols = slice(h * part, (h + 1) * part)
        return grads[spot(d, y_of, c), :, cols] + got_core[d, y_of, :, cols]

    def last_core(y_of):
        return send(
            grads.at[pl.ds(spot(0, y_of, 1 - c), n_outer), :, pl.ds(main, quarter)],
            last_got_core.at[y_of],
            all_sent,
            last_core_recv.at[y_of],
            partner,
            v,
        )

    def last_z(d):
        return send(
            last_send_z.at[d], last_got_z.at[z], all_sent, last_z_recv.at[z], at(d, y, c), v
        )

    def last_sum(d, y_of):
        return grads[spot(d, y_of, c), :, pl.ds(main, quarter)] + last_got_core[y_of, d]

    last_y = send(last_send_y, last_got_y, all_sent, last_y_recv, other_y, v)
    sent.append((0, n_outer, lambda k: [rs_core(k, 0), rs_core(k, 1)] + [rs_y(k, h) for h in range(PARTS)]))
    sent.append((1, n_outer, lambda k: [last_z(z)] + [rs_z(z, h) for h in range(PARTS)]))
    sent.append((0, 1, lambda k: (last_core(0), last_core(1), last_y)))

    rs_core(turn(0), 1 - y).start()
    for y_of in range(INNER):
        last_core(y_of).start()

    @pl.loop(1, n_outer)
    def _(n):
        rs_core(turn(n), 1 - y).start()

    @pl.loop(0, n_outer)
    def _(n):
        rs_core(turn(n), y).start()

    def send_other(n):
        d = turn(n)
        rs_core(d, 1 - y).wait_recv()
        for h in range(PARTS):
            send_y[d, h] = chip_sum(d, 1 - y, h)
            rs_y(d, h).start()

    send_other(0)
    for y_of in range(INNER):
        last_core(y_of).wait_recv()

    @pl.loop(0, n_outer - 1)
    def _(n):
        d = turn(n)
        for y_of in range(INNER):
            last_send_z[d, y_of] = last_sum(d, y_of)
        last_z(d).start()

    @pl.loop(1, n_outer)
    def _(n):
        send_other(n)

    @pl.loop(0, n_outer - 1)
    def _(n):
        d = turn(n)
        rs_core(d, y).wait_recv()
        for h in range(PARTS):
            rs_y(d, h).wait_recv()
            send_z[d, h] = chip_sum(d, y, h) + got_y[d, h]
            rs_z(d, h).start()

    last_own, last_other = last_sum(z, y), last_sum(z, 1 - y)
    for k in range(1, n_outer):
        z_from = fwd(k)
        got = last_got_z.at[z_from]
        send(got, got, all_sent, last_z_recv.at[z_from], dp, 1 - v).wait_recv()
        last_own = last_own + last_got_z[z_from, y]
        last_other = last_other + last_got_z[z_from, 1 - y]
    last_send_y[...] = last_other
    last_y.start()
    rs_core(z, y).wait_recv()
    row_halves = []
    for h in range(PARTS):
        rs_y(z, h).wait_recv()
        row_half = chip_sum(z, y, h) + got_y[z, h]
        for k in range(1, n_outer):
            z_from = fwd(k)
            got = got_z.at[z_from, h]
            send(got, got, all_sent, rs_z_recv.at[z_from, h], dp, 1 - v).wait_recv()
            row_half = row_half + got_z[z_from, h]
        row_halves.append(row_half)
    last_y.wait_recv()
    rows8 = jnp.concatenate([*row_halves, last_own + last_got_y[...]], axis=1)
    low, high = rows8[:own_rows], rows8[own_rows:]
    grad_near = jnp.where(v == 0, low, high)
    grad_far = jnp.where(v == 0, high, low)
    send_x[...] = grad_far
    x_copy = send(send_x, grad_x, all_sent, x_recv, dp, 1 - v)
    x_copy.start()
    sent.append((0, 1, lambda k: (x_copy,)))
    load_m.wait()
    load_v.wait()
    for copy in state_copies:
        copy.wait_recv()

    first_fix = 1.0 - BETA_ONE**STEP
    second_fix = 1.0 - BETA_TWO**STEP

    def lamb(grad, first, second):
        first = BETA_ONE * first + (1.0 - BETA_ONE) * grad
        second = BETA_TWO * second + (1.0 - BETA_TWO) * grad * grad
        update = first / first_fix / (jnp.sqrt(second / second_fix) + ADAM_EPSILON)
        return first, second, update

    def square_sum(values):
        return jnp.sum(values * values, axis=(0, 1), keepdims=True)

    def finish_half(grad, h):
        cols = pl.ds(pl.multiple_of(h * half, half), half)
        first, second, update = lamb(grad, m_buf[0, :, cols], v_buf[0, :, cols])
        new_m_ref[0, :, cols] = first
        new_v_ref[0, :, cols] = second
        update_buf[:, cols] = update
        return update

    lane = lax.broadcasted_iota(jnp.int32, (1, 128), 1)
    _, _, update_far = lamb(grad_far, state_far[0], state_far[1])
    sums_own[1] = jnp.where(lane == 0, square_sum(update_far), 0.0)
    def sum_far(to):
        return send(sums_own.at[1], sums.at[n_dp + dp], all_sent, sum_recv, to, 1 - v)

    def sum_near(to):
        return send(sums_own.at[0], sums.at[dp], all_sent, sum_recv, to, v)

    def near_dp(n):
        return jnp.where(z < n_outer // 2, n_dp - n, n)

    def to_dp(k):
        return lax.rem(dp + k, n_dp)

    @pl.loop(0, n_dp)
    def _(n):
        sum_far(to_dp(near_dp(n))).start()

    near = jnp.where(
        lane == 0,
        square_sum(finish_half(grad_near, v)),
        jnp.where(lane == 1, weight_part, 0.0),
    )
    sums_own[0] = near
    sums[dp] = near

    @pl.loop(1, n_dp)
    def _(n):
        sum_near(to_dp(near_dp(n))).start()

    sent.append((0, n_dp, lambda k: (sum_far(to_dp(k)),)))
    sent.append((1, n_dp, lambda k: (sum_near(to_dp(k)),)))
    x_copy.wait_recv()
    finish_half(grad_x[...], 1 - v)
    finish()
    arrivals = sums.at[pl.ds(0, 2 * n_dp - 1)]
    send(arrivals, arrivals, all_sent, sum_recv, dp, 1 - v).wait_recv()

    totals = jnp.sum(sums[...], axis=0)
    update_total = jnp.sum(jnp.where(lane == 0, totals, 0.0), axis=1, keepdims=True)
    weight_total = jnp.sum(jnp.where(lane == 1, totals, 0.0), axis=1, keepdims=True)
    trust = jnp.sqrt(weight_total) / (jnp.sqrt(update_total) + TRUST_EPSILON)
    new_head_ref[0] = head_ref[0] - LEARNING_RATE * trust * update_buf[...]


def store_kernel(*refs):
    count = (len(refs) - 1) // 2
    sems = refs[-1]
    copies = [
        pltpu.make_async_copy(refs[n], refs[count + n], sems.at[n]) for n in range(count)
    ]
    for copy in copies:
        copy.start()
    for copy in copies:
        copy.wait()


def fused_step(n_dp, hidden, positions, labels, lse_rest, head, m_state, v_state):
    seqs, length, half = hidden.shape
    masked = positions.shape[1]
    own_rows, width = head.shape[1], head.shape[2]
    n_outer = n_dp // (CORES * INNER)
    pair = 2 * own_rows
    quarter = half // 4
    block = n_dp * pair
    vmem = pl.BlockSpec(memory_space=pltpu.VMEM)
    anywhere = pl.BlockSpec(memory_space=pltpu.HBM)
    dma = pltpu.SemaphoreType.DMA
    state = jax.ShapeDtypeStruct(head.shape, F32)
    operands = [
        pltpu.with_memory_space_constraint(operand, pltpu.HBM)
        for operand in (hidden, positions, labels, lse_rest, head, m_state, v_state)
    ]
    results = pl.pallas_call(
        functools.partial(step_kernel, n_dp),
        out_shape=(jax.ShapeDtypeStruct(lse_rest.shape, F32), state, state, state),
        in_specs=[anywhere] * 7,
        out_specs=(vmem, vmem, vmem, vmem),
        scratch_shapes=[
            pltpu.VMEM((seqs, length, half), BF16),
            pltpu.VMEM((seqs, masked, half), BF16),
            pltpu.VMEM((n_dp, 2, own_rows, half), BF16),
            pltpu.VMEM((own_rows, half), BF16),
            pltpu.VMEM((INNER, max(seqs // 2, 1), masked, block), F32),
            pltpu.VMEM((INNER, max(seqs // 2, 1), masked, block), F32),
            pltpu.VMEM((INNER, masked // 2, block), F32),
            pltpu.VMEM((INNER, masked // 2, block), F32),
            pltpu.VMEM((n_dp, pair, half), F32),
            pltpu.VMEM((n_outer, INNER, pair, half - quarter), F32),
            pltpu.VMEM((INNER, n_outer, pair, quarter), F32),
            pltpu.VMEM((n_outer, INNER, pair, quarter), F32),
            pltpu.VMEM((n_outer, INNER, pair, quarter), F32),
            pltpu.VMEM((pair, quarter), F32),
            pltpu.VMEM((pair, quarter), F32),
            pltpu.VMEM((n_outer, PARTS, pair, (half - quarter) // PARTS), F32),
            pltpu.VMEM((n_outer, PARTS, pair, (half - quarter) // PARTS), F32),
            pltpu.VMEM((n_outer, PARTS, pair, (half - quarter) // PARTS), F32),
            pltpu.VMEM((n_outer, PARTS, pair, (half - quarter) // PARTS), F32),
            pltpu.VMEM((own_rows, half), F32),
            pltpu.VMEM((own_rows, half), F32),
            pltpu.VMEM((2, own_rows, half), F32),
            pltpu.VMEM((1, own_rows, width), F32),
            pltpu.VMEM((1, own_rows, width), F32),
            pltpu.VMEM(positions.shape, jnp.int32),
            pltpu.VMEM(labels.shape, jnp.int32),
            pltpu.VMEM(lse_rest.shape, F32),
            pltpu.VMEM(head.shape, F32),
            pltpu.VMEM((own_rows, width), F32),
            pltpu.VMEM((2, 1, 128), F32),
            pltpu.VMEM((2 * n_dp, 1, 128), F32),
            dma((seqs,)),
            dma((6,)),
            dma,
            dma,
            dma((n_outer, 2)),
            dma((n_outer,)),
            dma((INNER,)),
            dma((INNER, max(seqs // 2, 1))),
            dma((INNER,)),
            dma((n_outer, INNER)),
            dma((INNER,)),
            dma((n_outer,)),
            dma,
            dma((n_outer, PARTS)),
            dma((n_outer, PARTS)),
            dma,
            dma,
            dma((2,)),
        ],
        compiler_params=pltpu.CompilerParams(
            collective_id=0, has_side_effects=True, vmem_limit_bytes=48 * 1024 * 1024
        ),
        name="fused_step",
    )(*operands)
    count = len(results)
    return pl.pallas_call(
        store_kernel,
        out_shape=tuple(jax.ShapeDtypeStruct(r.shape, r.dtype) for r in results),
        in_specs=[vmem] * count,
        out_specs=(anywhere,) * count,
        scratch_shapes=[dma((count,))],
        compiler_params=pltpu.CompilerParams(vmem_limit_bytes=4 * 1024 * 1024),
        name="store_results",
    )(*results)


def on_device(hidden, positions, labels, lse_rest, head, m_state, v_state):
    seq_here, mask_here = positions.shape
    rows_here = seq_here * mask_here
    own_rows = head.shape[1]
    model_width = head.shape[2]
    head_own = head.reshape(own_rows, model_width)
    weight_total = lax.psum(jnp.sum(head_own * head_own), "dp")
    local_rows = jnp.take_along_axis(hidden, positions[:, :, None], axis=1).reshape(
        rows_here, hidden.shape[2]
    )
    picked = lax.all_gather(local_rows, "vocab", axis=1, tiled=True)
    head_copy = head_own.astype(jnp.bfloat16)
    scores = lax.dot_general(
        picked,
        lax.all_gather(head_copy, "dp", axis=0, tiled=True),
        (((1,), (1,)), ((), ())),
        preferred_element_type=jnp.float32,
    )
    slab_width = scores.shape[1]
    offset = lax.axis_index("vocab") * slab_width
    label_local = labels.reshape(rows_here) - offset
    label_hits = label_local[:, None] == lax.iota(jnp.int32, slab_width)[None, :]
    target_part = jnp.sum(jnp.where(label_hits, scores, 0.0), axis=1)
    rest_lse = lse_rest.reshape(rows_here)
    slab_max = jnp.max(scores, axis=1)
    block_max = lax.pmax(slab_max, "vocab")
    row_top = jnp.maximum(block_max, rest_lse)
    slab_sum = jnp.sum(jnp.exp(scores - row_top[:, None]), axis=1)
    block_sum, target = lax.psum((slab_sum, target_part), "vocab")
    row_total = block_sum + jnp.exp(rest_lse - row_top)
    row_lse = row_top + jnp.log(row_total)
    losses = (row_lse - target).reshape(seq_here, mask_here)
    logit_grad = (jnp.exp(scores - row_lse[:, None]) - label_hits.astype(jnp.float32)).astype(
        jnp.bfloat16
    )
    full_grad = lax.dot_general(
        logit_grad, picked, (((0,), (0,)), ((), ())), preferred_element_type=jnp.float32
    )
    head_grad = lax.psum_scatter(full_grad, "dp", scatter_dimension=0, tiled=True)
    first_moment = BETA_ONE * m_state.reshape(own_rows, model_width) + (1.0 - BETA_ONE) * head_grad
    second_moment = (
        BETA_TWO * v_state.reshape(own_rows, model_width) + (1.0 - BETA_TWO) * head_grad * head_grad
    )
    first_fix = 1.0 - BETA_ONE**STEP
    second_fix = 1.0 - BETA_TWO**STEP
    update = first_moment / first_fix / (jnp.sqrt(second_moment / second_fix) + ADAM_EPSILON)
    update_part = jnp.sum(update * update)
    update_total = lax.psum(update_part, "dp")
    trust_ratio = jnp.sqrt(weight_total) / (jnp.sqrt(update_total) + TRUST_EPSILON)
    new_head = head_own - LEARNING_RATE * trust_ratio * update
    return (
        losses,
        new_head.reshape(head.shape),
        first_moment.reshape(head.shape),
        second_moment.reshape(head.shape),
    )


def pairwise(mesh, args):
    n_dp, n_vocab = mesh.shape["dp"], mesh.shape["vocab"]
    own_rows = args[4].shape[1] // n_dp
    power_of_two = own_rows & (own_rows - 1) == 0
    n_outer = n_dp // (CORES * INNER)
    power_of_two = power_of_two and n_outer & (n_outer - 1) == 0
    masked, width = args[1].shape[1], args[4].shape[2]
    power_of_two = power_of_two and masked % 16 == 0 and width % 2048 == 0
    return n_vocab == 2 and n_dp % (CORES * INNER) == 0 and power_of_two


def solution(mesh):
    def step(*args):
        if pairwise(mesh, args):
            body = functools.partial(fused_step, mesh.shape["dp"])
        else:
            body = on_device
        return sharded(mesh, body)(*args)

    return step


def sharded(mesh, body):
    return jax.shard_map(
        body,
        mesh=mesh,
        in_specs=(
            P("dp", None, "vocab"),
            P("dp", None),
            P("dp", None),
            P("dp", None),
            P("vocab", "dp", None),
            P("vocab", "dp", None),
            P("vocab", "dp", None),
        ),
        out_specs=(
            P("dp", None),
            P("vocab", "dp", None),
            P("vocab", "dp", None),
            P("vocab", "dp", None),
        ),
        check_vma=False,
    )
```
